128 devices in a mesh: aux: 4 (over y), tile: 32 (over x, z, core).
Axes of the slice: x: 4, y: 4, z: 4, core: 2. Of those that a mesh axis runs over, the one named last changes fastest.
Arguments:
- integrals: bfloat16 [11904, 8, 2944], P(('aux', 'tile')), may hold values from -0.57421875 to 0.57421875
- coefficients: bfloat16 [2944, 2048], replicated, may hold values from -0.109375 to 0.109375
- owned_tiles: int32 [2, 64], replicated, may hold values from 0 to 63, each once within a row
- pair_list: int32 [2, 64, 4], P(None, 'tile'), may hold values from -1 to 63, as said below
- amplitudes: bfloat16 [2, 64, 4, 128, 128], P(None, 'tile'), may hold values from -0.25 to 0.25
Outputs:
- residual: float32 [2, 64, 128, 128], P(None, 'tile')
The draws below stay inside these ranges and needn't reach their ends.
Inputs may be any that keep to these rules, and one draw needn't show every extreme that they name: `pair_list`: every live entry of slot s is a slot within 2 of s; the live entries of one slot are distinct; -1 marks an entry dropped by screening.
All inputs are finite; a program needn't handle non-finite values.
Results may differ from the reference program's by a relative error of at most 0.00087.
Values may be sent and summed in bfloat16 or wider, within the bound.
A program may use at most 128 MiB of HBM per device.

```python
import jax
import jax.numpy as jnp
from jax import lax

NAUX = 11904
NAO = 2944
TILE = 128
NVT = 16
NB = 2
NPART = 4
PTD = 2
NV = 2048
PT = 64
NOCC = 8


def draw_pair_list(key, part):
    offsets = 2 * PTD + 1
    keys = jax.random.split(jax.random.fold_in(key, 11), NB * PT)
    perms = jax.vmap(lambda one_key: jax.random.permutation(one_key, offsets))(keys)
    picked = perms[:, :NPART].reshape(NB, PT, NPART).astype(jnp.int32) - PTD
    slots = jnp.arange(PT, dtype=jnp.int32)[None, :, None]
    target = slots + picked
    dropped = jax.random.randint(jax.random.fold_in(key, 23), (NB, PT, NPART), 0, 4) == 0
    valid = (target >= 0) & (target < PT) & jnp.logical_not(dropped)
    return jnp.where(valid, target, -1).astype(jnp.int32)


def block_scale(key, shape, pieces, low, top_value):
    def one(dim, parts):
        heights = jax.random.uniform(jax.random.fold_in(jax.random.fold_in(key, 6), dim), (parts,), jnp.float32, low / len(pieces), top_value / len(pieces))
        return jnp.repeat(jnp.exp(heights), shape[dim] // parts).reshape((-1,) + (1,) * (len(shape) - dim - 1))

    loudness = one(*pieces[0])
    for cut in pieces[1:]:
        loudness = loudness * one(*cut)
    return loudness


def centred(rng, extent, deviation, most, cuts=(), held_as=jnp.bfloat16):
    values = jax.random.normal(rng, extent, jnp.float32) * deviation
    if len(cuts) > 0:
        values = block_scale(rng, extent, cuts, -0.22, 0.18) * values
    return jnp.clip(values, min=-most, max=most).astype(held_as)


def setup_inputs(seed: int = 0) -> dict:
    key_list = jax.random.split(jax.random.key(seed), 6)
    return {
        "integrals": centred(key_list[0], (NAUX, NOCC, NAO), (NAUX ** -0.25), 0.57421875, ((0, 128),)),
        "coefficients": centred(key_list[1], (NAO, NV), NAO ** -0.5, 0.109375),
        "owned_tiles": jax.vmap(lambda own: jax.random.permutation(own, PT))(jax.random.split(key_list[2], NB)).reshape((NB, PT)).astype(jnp.int32),
        "pair_list": draw_pair_list(jax.random.fold_in(key_list[5], 71), 0),
        "amplitudes": centred(key_list[4], (NB, PT, NPART, TILE, TILE), (TILE * NPART) ** -0.5, 0.25, ((1, 32),)),
    }


def reference(integrals, coefficients, owned_tiles, pair_list, amplitudes):
    occ_batch = integrals.shape[1] // NB
    results = []
    for occ_group in range(NB):
        int_block = integrals[:, occ_group * occ_batch:(occ_group + 1) * occ_batch, :].reshape(NAUX * occ_batch, NAO)
        half_done = jnp.dot(int_block, coefficients, preferred_element_type=jnp.float32).astype(jnp.bfloat16)
        half_done = half_done.reshape(NAUX, occ_batch * NVT, TILE)
        ordered = jnp.take(half_done, owned_tiles[occ_group], axis=1)

        def one_slot(slot_idx):
            mine = lax.dynamic_index_in_dim(ordered, slot_idx, 1, keepdims=False).astype(jnp.float32)
            listed = pair_list[occ_group, slot_idx]
            live_mask = (listed >= 0).astype(jnp.float32)
            others = jnp.take(ordered, jnp.maximum(listed, 0), axis=1).astype(jnp.float32)
            pair_ints = jnp.einsum("qa,qkb->kab", mine, others, precision=lax.Precision.HIGHEST)
            pair_ints = pair_ints * live_mask[:, None, None]
            amp_tiles = amplitudes[occ_group, slot_idx].astype(jnp.float32)
            return jnp.einsum("kab,kbc->ac", pair_ints, amp_tiles, precision=lax.Precision.HIGHEST)

        results.append(lax.map(one_slot, jnp.arange(PT, dtype=jnp.int32)))
    return jnp.stack(results)
```

```python
import functools

import jax
import jax.numpy as jnp
from jax import lax
from jax.experimental import pallas as pl
from jax.experimental.pallas import tpu as pltpu
from jax.sharding import PartitionSpec as P

MESH = pl.DeviceIdType.MESH
F32 = jnp.float32
BF16 = jnp.bfloat16

NB = 2
T = 128
NT = 64
NOCC = 8
NOFF = 5
BLK = 16
WIN = BLK + 4
CH = 48
NCH = 2
NSRC = 8
CB = 256


def dev(x, y, z, c):
    return (y, x * 8 + z * 2 + c)


def remote(src, dst, ssem, rsem, where):
    return pltpu.make_async_remote_copy(
        src_ref=src, dst_ref=dst, send_sem=ssem, recv_sem=rsem, device_id=where, device_id_type=MESH
    )


def kernel(
    q_rows,
    owned, plist, integ, coef, amp, out,
    lhs, cbuf, acc, ynat, send, recv, rr, amp5, ampbuf, res, rsrecv, ysend, yrecv, fsend,
    lsem, csem, gsend, grecv, f1send, f1recv, f2send, f2recv, rssend, rsrecv_sem, yssend, ysrecv,
    fssend, fsrecv, locsem,
):
    y = lax.axis_index("aux")
    t = lax.axis_index("tile")
    x = t // 8
    z = (t // 2) % 4
    c = t % 2
    l = x * (1 - c) + z * c
    o = z * (1 - c) + x * c
    nblk = coef.shape[1] // CB
    tail = q_rows - CH

    def lhs_copy(h):
        rows = (CH if h == 0 else tail) * NOCC
        return pltpu.make_async_copy(
            integ.at[pl.ds(h * CH * NOCC, rows)], lhs.at[h, pl.ds(0, rows)], lsem.at[h]
        )

    def coef_copy(n):
        return pltpu.make_async_copy(
            coef.at[:, pl.ds(pl.multiple_of(n * CB, CB), CB)], cbuf.at[n], csem.at[n]
        )

    lhs_copy(0).start()
    for n in range(nblk):
        coef_copy(n).start()
    lhs_copy(1).start()

    bar = pltpu.get_barrier_semaphore()

    def greet(k, carry):
        pl.semaphore_signal(bar, inc=1, device_id=(y, (t + k) % 32), device_id_type=MESH)
        return carry

    lax.fori_loop(1, 32, greet, 0)
    for d in range(1, 4):
        for cc in range(2):
            pl.semaphore_signal(bar, inc=1, device_id=dev(x, (y + d) % 4, z, cc), device_id_type=MESH)
            pl.semaphore_signal(bar, inc=1, device_id=dev(z, (y + d) % 4, x, cc), device_id_type=MESH)

    for b in range(NB):
        for j in range(2):
            slot = 2 * t + j
            for off in range(NOFF):
                total = jnp.zeros((T, T), F32)
                for k in range(4):
                    p = plist[(b * 2 + j) * 4 + k]
                    hit = jnp.logical_and(p >= 0, p - slot + 2 == off).astype(F32)
                    total = total + hit * amp[b, j, k].astype(F32)
                amp5[b, j, off] = total.astype(BF16)

    pl.semaphore_wait(bar, 43)

    quarter = pl.ds(pl.multiple_of(y * 32, 32), 32)
    me8 = z * 2 + c
    f1 = []
    for d in range(4):
        f1.append((0, d, dev(x, y, (z + d) % 4, 0), (c == 0) if d == 0 else None))
        f1.append((1, d, dev((x + d) % 4, y, x, 1), ((c == 1) & (z == x)) if d == 0 else None))

    def f1_copies(i):
        b, d, where, is_self = f1[i]
        src = amp5.at[b, :, :, quarter]
        dst = ampbuf.at[pl.ds(me8 * 2, 2), :, quarter]
        far = remote(src, dst, f1send.at[i], f1recv.at[me8], where)
        near = pltpu.make_async_copy(src, dst, f1recv.at[me8])
        return far, near, is_self

    def start_either(copies):
        far, near, is_self = copies
        if is_self is None:
            far.start()
        else:
            @pl.when(is_self)
            def _():
                near.start()

            @pl.when(jnp.logical_not(is_self))
            def _():
                far.start()

    def finish_send(copies):
        far, near, is_self = copies
        if is_self is None:
            far.wait_send()
        else:
            @pl.when(jnp.logical_not(is_self))
            def _():
                far.wait_send()

    for i in range(8):
        start_either(f1_copies(i))

    here = dev(x, y, z, c)

    def half(h, n):
        whole = jnp.dot(lhs[h], cbuf[n], preferred_element_type=F32)
        for a in range(CB // T):
            acc[a] = whole[:, a * T : (a + 1) * T]
        for i in range(NOCC):
            for a in range(CB // T):
                part = acc[a, pl.ds(i, CH, stride=NOCC), :]
                if h == NCH - 1:
                    rows = lax.broadcasted_iota(jnp.int32, (CH, T), 0)
                    part = jnp.where(rows < tail, part, 0.0)
                ynat[i // 4, (i % 4) * 16 + 2 * n + a] = part.astype(BF16)

    def reorder(h):
        for b in range(NB):
            def one(s, carry):
                send[h, b, s] = ynat[b, owned[b * NT + (s + NT - 2) % NT]]
                return carry

            lax.fori_loop(0, NT + 4, one, 0, unroll=4)

    def place(k):
        return pl.ds(pl.multiple_of(k * CH, CH), CH)

    def gather_copies(h):
        out_copies = []
        for d in range(1, 4):
            xd, zd = (x + d) % 4, (z + d) % 4
            for b, at, k, where in (
                (0, xd, x * 2 + c, dev(xd, y, z, 0)),
                (1, zd, z * 2 + c, dev(x, y, zd, 1)),
            ):
                out_copies.append(
                    remote(
                        send.at[h, b, pl.ds(at * BLK, WIN)],
                        recv.at[h, :, place(k)],
                        gsend.at[h, len(out_copies)],
                        grecv.at[h, k],
                        where,
                    )
                )
        out_copies.append(
            remote(
                send.at[h, 1 - c, pl.ds(o * BLK, WIN)],
                recv.at[h, :, place(o * 2 + c)],
                gsend.at[h, 6],
                grecv.at[h, o * 2 + c],
                dev(x, y, z, 1 - c),
            )
        )
        own = pltpu.make_async_copy(
            send.at[h, c, pl.ds(l * BLK, WIN)], recv.at[h, :, place(l * 2 + c)], locsem.at[h]
        )
        return out_copies, own

    def gather_start(h):
        out_copies, own = gather_copies(h)
        for copy in out_copies:
            copy.start()
        own.start()

    def gather_wait(h):
        out_copies, own = gather_copies(h)
        own.wait()

        def arrived(k):
            remote(
                send.at[h, 0, pl.ds(0, WIN)], recv.at[h, :, place(k)], gsend.at[h, 0], grecv.at[h, k], here
            ).wait_recv()

        arrived(l * 2 + 1 - c)
        for d in range(1, 4):
            for cc in range(2):
                arrived(((l + d) % 4) * 2 + cc)

    def pairs(h):
        def one(j, carry):
            mine = jnp.concatenate([recv[h, 2 * j + 2], recv[h, 2 * j + 3]], axis=1)
            others = jnp.concatenate([recv[h, 2 * j + m] for m in range(6)], axis=1)
            got = lax.dot_general(
                mine, others, (((0,), (0,)), ((), ())), preferred_element_type=F32
            )
            if h == 0:
                rr[j] = got
            else:
                rr[j] = rr[j] + got
            return carry

        lax.fori_loop(0, BLK // 2, one, 0)

    def block0(n, carry):
        coef_copy(n).wait()
        half(0, n)
        return carry

    def block1(n, carry):
        half(1, n)
        return carry

    lhs_copy(0).wait()
    lax.fori_loop(0, nblk // 2, block0, 0)

    f2 = []
    for k in range(NSRC):
        remote(
            amp5.at[0, :, :, quarter], ampbuf.at[pl.ds(2 * k, 2), :, quarter], f1send.at[0], f1recv.at[k], here
        ).wait_recv()
    for d in range(1, 4):
        f2.append(
            remote(
                ampbuf.at[:, :, quarter], ampbuf.at[:, :, quarter], f2send.at[d - 1], f2recv.at[d - 1],
                dev(x, (y + d) % 4, z, c),
            )
        )
        f2[-1].start()

    lax.fori_loop(nblk // 2, nblk, block0, 0)
    reorder(0)
    gather_start(0)
    lhs_copy(1).wait()
    lax.fori_loop(0, nblk, block1, 0)
    reorder(1)
    gather_start(1)
    gather_wait(0)
    pairs(0)
    for d in range(1, 4):
        far_quarter = pl.ds(pl.multiple_of(((y + 4 - d) % 4) * 32, 32), 32)
        remote(
            ampbuf.at[:, :, far_quarter], ampbuf.at[:, :, far_quarter], f2send.at[d - 1], f2recv.at[d - 1], here
        ).wait_recv()
    gather_wait(1)
    pairs(1)

    def contract(op):
        for jj in range(2):
            j = op * 2 + jj
            for e in range(2):
                whole = rr[j, pl.ds(e * T, T), pl.ds(e * T, NOFF * T)]
                high = whole.astype(BF16)
                low = (whole - high.astype(F32)).astype(BF16)
                weights = jnp.concatenate([ampbuf[2 * j + e, m] for m in range(NOFF)], axis=0)
                res[2 * j + e] = jnp.dot(high, weights, preferred_element_type=F32) + jnp.dot(
                    low, weights, preferred_element_type=F32
                )

    rs = []
    for d in range(1, 4):
        op = (o + d) % 4
        contract(op)
        rs.append(
            remote(
                res.at[pl.ds(op * 4, 4)], rsrecv.at[d - 1], rssend.at[d - 1], rsrecv_sem.at[d - 1],
                dev((x + d * c) % 4, y, (z + d * (1 - c)) % 4, c),
            )
        )
        rs[-1].start()
    contract(o)
    for copy in rs:
        copy.wait_recv()

    ys = []
    for d in range(1, 5):
        j = (y + d) % 4
        ysend[d - 1] = (res[o * 4 + j] + rsrecv[0, j]) + (rsrecv[1, j] + rsrecv[2, j])
        if d < 4:
            ys.append(
                remote(
                    ysend.at[d - 1], yrecv.at[d - 1], yssend.at[d - 1], ysrecv.at[d - 1],
                    dev(x, j, z, c),
                )
            )
            ys[-1].start()
    for copy in ys:
        copy.wait_recv()
    fsend[...] = (ysend[3] + yrecv[0]) + (yrecv[1] + yrecv[2])

    def final_copies(d):
        dst = out.at[c, y % 2]
        where = dev(l, (y + d) % 4, o, y // 2)
        far = remote(fsend, dst, fssend.at[d], fsrecv.at[c * 2 + y % 2], where)
        near = pltpu.make_async_copy(fsend, dst, fsrecv.at[c * 2 + y % 2])
        is_self = ((y // 2 == c) & (l == x) & (o == z)) if d == 0 else None
        return far, near, is_self

    for d in range(4):
        start_either(final_copies(d))
    for b in range(NB):
        for j in range(2):
            remote(fsend, out.at[b, j], fssend.at[0], fsrecv.at[b * 2 + j], here).wait_recv()

    for i in range(8):
        finish_send(f1_copies(i))
    for copy in f2 + rs + ys:
        copy.wait_send()
    for h in range(NCH):
        for copy in gather_copies(h)[0]:
            copy.wait_send()
    for d in range(4):
        finish_send(final_copies(d))


def per_device(integrals, coefficients, owned_tiles, pair_list, amplitudes):
    q_rows, occ, ao = integrals.shape
    nv = coefficients.shape[1]
    dma = pltpu.SemaphoreType.DMA
    vmem = pl.BlockSpec(memory_space=pltpu.VMEM)
    smem = pl.BlockSpec(memory_space=pltpu.SMEM)
    hbm = pl.BlockSpec(memory_space=pl.ANY)
    return pl.pallas_call(
        functools.partial(kernel, q_rows),
        out_shape=jax.ShapeDtypeStruct((NB, 2, T, T), F32),
        in_specs=[smem, smem, hbm, hbm, vmem],
        out_specs=vmem,
        scratch_shapes=[
            pltpu.VMEM((NCH, CH * NOCC, ao), BF16),
            pltpu.VMEM((nv // CB, ao, CB), BF16),
            pltpu.VMEM((CB // T, CH * NOCC, T), F32),
            pltpu.VMEM((NB, NT, CH, T), BF16),
            pltpu.VMEM((NCH, NB, NT + 4, CH, T), BF16),
            pltpu.VMEM((NCH, WIN, NSRC * CH, T), BF16),
            pltpu.VMEM((BLK // 2, 2 * T, 6 * T), F32),
            pltpu.VMEM((NB, 2, NOFF, T, T), BF16),
            pltpu.VMEM((BLK, NOFF, T, T), BF16),
            pltpu.VMEM((BLK, T, T), F32),
            pltpu.VMEM((3, 4, T, T), F32),
            pltpu.VMEM((4, T, T), F32),
            pltpu.VMEM((3, T, T), F32),
            pltpu.VMEM((T, T), F32),
            dma((NCH,)),
            dma((nv // CB,)),
            dma((NCH, 7)),
            dma((NCH, NSRC)),
            dma((8,)),
            dma((NSRC,)),
            dma((3,)),
            dma((3,)),
            dma((3,)),
            dma((3,)),
            dma((3,)),
            dma((3,)),
            dma((4,)),
            dma((4,)),
            dma((NCH,)),
        ],
        compiler_params=pltpu.CompilerParams(
            collective_id=0, has_side_effects=True, vmem_limit_bytes=60 * 2**20
        ),
        name="residual_kernel",
    )(
        owned_tiles.reshape(-1),
        pair_list.reshape(-1),
        integrals.reshape(q_rows * occ, ao),
        coefficients,
        amplitudes,
    )


def solution(mesh):
    in_specs = (
        P(("aux", "tile"), None, None),
        P(),
        P(),
        P(None, "tile", None),
        P(None, "tile", None, None, None),
    )
    out_specs = P(None, "tile", None, None)
    return jax.shard_map(
        per_device, mesh=mesh, in_specs=in_specs, out_specs=out_specs, check_vma=False
    )
```

```python
import functools

import jax
import jax.numpy as jnp
from jax import lax
from jax.experimental import pallas as pl
from jax.experimental.pallas import tpu as pltpu
from jax.sharding import PartitionSpec as P

MESH = pl.DeviceIdType.MESH
F32 = jnp.float32
BF16 = jnp.bfloat16

NB = 2
T = 128
NT = 64
NOCC = 8
NOFF = 5
BLK = 16
WIN = BLK + 4
CH = 32
NCH = 3
NSRC = 8
CB = 256
QR = T // 4


def dev(x, y, z, c):
    return (y, x * 8 + z * 2 + c)


def remote(src, dst, ssem, rsem, where):
    return pltpu.make_async_remote_copy(
        src_ref=src, dst_ref=dst, send_sem=ssem, recv_sem=rsem, device_id=where, device_id_type=MESH
    )


def kernel(
    q_rows,
    owned, plist, integ, coef, amp, out,
    lhs, cbuf, acc, ynat, send, recv, rr, amp5, ampbuf, res, rsgot, ysend, ygot, fsend,
    lsem, csem, gsend, grecv, f1send, f1recv, f2send, f2recv, rssend, rsrecv, yssend, ysrecv,
    fssend, fsrecv, locsem,
):
    y = lax.axis_index("aux")
    t = lax.axis_index("tile")
    x = t // 8
    z = (t // 2) % 4
    c = t % 2
    l = x * (1 - c) + z * c
    o = z * (1 - c) + x * c
    here = dev(x, y, z, c)
    nblk = coef.shape[1] // CB
    tail = q_rows - (NCH - 1) * CH

    def lhs_copy(h):
        rows = (CH if h < NCH - 1 else tail) * NOCC
        return pltpu.make_async_copy(
            integ.at[pl.ds(h * CH * NOCC, rows)], lhs.at[h, pl.ds(0, rows)], lsem.at[h]
        )

    def coef_copy(n):
        return pltpu.make_async_copy(
            coef.at[:, pl.ds(pl.multiple_of(n * CB, CB), CB)], cbuf.at[n], csem.at[n]
        )

    lhs_copy(0).start()
    for n in range(nblk):
        coef_copy(n).start()
    for h in range(1, NCH):
        lhs_copy(h).start()

    bar = pltpu.get_barrier_semaphore()

    def greet_plane(k, carry):
        pl.semaphore_signal(bar, inc=1, device_id=(y, (t + k) % 32), device_id_type=MESH)
        return carry

    def greet_others(k, carry):
        yy = (y + 1 + k // 8) % 4
        pl.semaphore_signal(bar, inc=1, device_id=(yy, x * 8 + k % 8), device_id_type=MESH)
        pl.semaphore_signal(
            bar, inc=1, device_id=dev((k // 2) % 4, yy, x, k % 2), device_id_type=MESH
        )
        return carry

    lax.fori_loop(1, 32, greet_plane, 0)
    lax.fori_loop(0, 24, greet_others, 0)

    for b in range(NB):
        for j in range(2):
            slot = 2 * t + j
            for off in range(NOFF):
                total = jnp.zeros((T, T), F32)
                for k in range(4):
                    p = plist[b, j, k]
                    hit = jnp.logical_and(p >= 0, p - slot + 2 == off).astype(F32)
                    total = total + hit * amp[b, j, k].astype(F32)
                amp5[b, j, off] = total.astype(BF16)

    def start_either(copies):
        far, near, is_self = copies
        if is_self is None:
            far.start()
        else:

            @pl.when(is_self)
            def _():
                near.start()

            @pl.when(jnp.logical_not(is_self))
            def _():
                far.start()

    def finish_send(copies):
        far, near, is_self = copies
        if is_self is None:
            far.wait_send()
        else:

            @pl.when(jnp.logical_not(is_self))
            def _():
                far.wait_send()

    def quarter_of(yy):
        return pl.ds(pl.multiple_of(yy * QR, QR), QR)

    quarter = quarter_of(y)
    me8 = z * 2 + c

    def f1_copies(b, d):
        src = amp5.at[b, :, :, quarter]
        dst = ampbuf.at[pl.ds(me8 * 2, 2), :, quarter]
        if b == 0:
            where, is_self = dev(x, y, (z + d) % 4, 0), c == 0
        else:
            where, is_self = dev((x + d) % 4, y, x, 1), (c == 1) & (z == x)
        far = remote(src, dst, f1send.at[b, d], f1recv.at[me8], where)
        near = pltpu.make_async_copy(src, dst, f1recv.at[me8])
        return far, near, is_self if d == 0 else None

    def f2_copy(g, d, yy, where):
        part = ampbuf.at[pl.ds(4 * g, 4), :, quarter_of(yy)]
        return remote(part, part, f2send.at[g, d - 1], f2recv.at[g, d - 1], where)

    def f2_start(g):
        for k in (2 * g, 2 * g + 1):
            remote(
                amp5.at[0, :, :, quarter], ampbuf.at[pl.ds(2 * k, 2), :, quarter],
                f1send.at[0, 0], f1recv.at[k], here,
            ).wait_recv()
        for d in range(1, 4):
            f2_copy(g, d, y, dev(x, (y + d) % 4, z, c)).start()

    def half(h, n):
        whole = jnp.dot(lhs[h], cbuf[n], preferred_element_type=F32)
        for a in range(CB // T):
            acc[a] = whole[:, a * T : (a + 1) * T]
        for i in range(NOCC):
            for a in range(CB // T):
                part = acc[a, pl.ds(i, CH, stride=NOCC), :]
                if h == NCH - 1:
                    rows = lax.broadcasted_iota(jnp.int32, (CH, T), 0)
                    part = jnp.where(rows < tail, part, 0.0)
                ynat[i // 4, (i % 4) * 16 + 2 * n + a] = part.astype(BF16)

    def reorder(h):
        for b in range(NB):

            def one(s, carry):
                send[h, b, s] = ynat[b, owned[b, (s + NT - 2) % NT]]
                return carry

            lax.fori_loop(0, NT + 4, one, 0, unroll=4)

    def place(k):
        return pl.ds(pl.multiple_of(k * CH, CH), CH)

    def groups(h):
        return ((0, 8), (8, 4), (12, 4), (16, 4)) if h == NCH - 1 else ((0, WIN),)

    def gather_copies(h, g):
        low, count = groups(h)[g]
        q = h + g
        copies = []
        for d in range(1, 4):
            xd, zd = (x + d) % 4, (z + d) % 4
            for b, at, k, where in (
                (0, xd, x * 2 + c, dev(xd, y, z, 0)),
                (1, zd, z * 2 + c, dev(x, y, zd, 1)),
            ):
                copies.append(
                    remote(
                        send.at[h, b, pl.ds(at * BLK + low, count)],
                        recv.at[h, pl.ds(low, count), place(k)],
                        gsend.at[q, len(copies)],
                        grecv.at[q, k],
                        where,
                    )
                )
        copies.append(
            remote(
                send.at[h, 1 - c, pl.ds(o * BLK + low, count)],
                recv.at[h, pl.ds(low, count), place(o * 2 + c)],
                gsend.at[q, 6],
                grecv.at[q, o * 2 + c],
                dev(x, y, z, 1 - c),
            )
        )
        own = pltpu.make_async_copy(
            send.at[h, c, pl.ds(l * BLK + low, count)],
            recv.at[h, pl.ds(low, count), place(l * 2 + c)],
            locsem.at[q],
        )
        return copies, own

    def gather_start(h):
        for g in range(len(groups(h))):
            copies, own = gather_copies(h, g)
            for copy in copies:
                copy.start()
            own.start()

    def gather_wait(h, g):
        low, count = groups(h)[g]
        q = h + g
        gather_copies(h, g)[1].wait()

        def arrived(k):
            remote(
                send.at[h, 0, pl.ds(low, count)], recv.at[h, pl.ds(low, count), place(k)],
                gsend.at[q, 0], grecv.at[q, k], here,
            ).wait_recv()

        arrived(l * 2 + 1 - c)
        for d in range(1, 4):
            for cc in range(2):
                arrived(((l + d) % 4) * 2 + cc)

    def pairs(h, first, last):
        def one(j, carry):
            mine = jnp.concatenate([recv[h, 2 * j + 2], recv[h, 2 * j + 3]], axis=1)
            others = jnp.concatenate([recv[h, 2 * j + m] for m in range(6)], axis=1)
            got = lax.dot_general(
                mine, others, (((0,), (0,)), ((), ())), preferred_element_type=F32
            )
            if h == 0:
                rr[j] = got
            else:
                rr[j] = rr[j] + got
            return carry

        lax.fori_loop(first, last, one, 0)

    def contract(g):
        for e in range(4):
            j, u = 2 * g + e // 2, e % 2
            whole = rr[j, pl.ds(u * T, T), pl.ds(u * T, NOFF * T)]
            high = whole.astype(BF16)
            low = (whole - high.astype(F32)).astype(BF16)
            weights = jnp.concatenate([ampbuf[4 * g + e, m] for m in range(NOFF)], axis=0)
            res[4 * g + e] = jnp.dot(high, weights, preferred_element_type=F32) + jnp.dot(
                low, weights, preferred_element_type=F32
            )

    def rs_copy(g, d):
        return remote(
            res.at[4 * g + (o + d) % 4], rsgot.at[g, d - 1], rssend.at[g, d - 1], rsrecv.at[g, d - 1],
            dev((x + d * c) % 4, y, (z + d * (1 - c)) % 4, c),
        )

    def y_copy(g, d):
        return remote(
            ysend.at[g, quarter_of((y + d) % 4)], ygot.at[g, d - 1], yssend.at[g, d - 1],
            ysrecv.at[g, d - 1], dev(x, (y + d) % 4, z, c),
        )

    def y_start(g):
        for d in range(1, 4):
            rs_copy(g, d).wait_recv()
        ysend[g] = (res[4 * g + o] + rsgot[g, 0]) + (rsgot[g, 1] + rsgot[g, 2])
        for d in range(1, 4):
            y_copy(g, d).start()

    def final_copies(g, d):
        dst = out.at[c, o % 2, quarter]
        sem = fsrecv.at[c * 8 + (o % 2) * 4 + y]
        far = remote(fsend.at[g], dst, fssend.at[g, d], sem, dev(l, (y + d) % 4, g, o // 2))
        near = pltpu.make_async_copy(fsend.at[g], dst, sem)
        is_self = ((o // 2 == c) & (l == x) & (z == g)) if d == 0 else None
        return far, near, is_self

    def final_start(g):
        for d in range(1, 4):
            y_copy(g, d).wait_recv()
        fsend[g] = (ysend[g, quarter] + ygot[g, 0]) + (ygot[g, 1] + ygot[g, 2])
        for d in range(4):
            start_either(final_copies(g, d))

    def block(h):
        def one(n, carry):
            if h == 0:
                coef_copy(n).wait()
            half(h, n)
            return carry

        return one

    lhs_copy(0).wait()
    lax.fori_loop(0, nblk // 2, block(0), 0)
    pl.semaphore_wait(bar, 31 + 48)
    for d in range(4):
        for b in range(NB):
            start_either(f1_copies(b, d))
    lax.fori_loop(nblk // 2, nblk, block(0), 0)
    reorder(0)
    gather_start(0)
    lhs_copy(1).wait()
    lax.fori_loop(0, nblk, block(1), 0)
    reorder(1)
    gather_start(1)
    for g in range(4):
        f2_start(g)
    lhs_copy(2).wait()
    lax.fori_loop(0, nblk, block(2), 0)
    reorder(2)
    gather_start(2)
    for h in range(NCH - 1):
        gather_wait(h, 0)
        pairs(h, 0, BLK // 2)
    for g in range(6):
        if g < 4:
            gather_wait(NCH - 1, g)
            pairs(NCH - 1, 2 * g, 2 * g + 2)
            for d in range(1, 4):
                f2_copy(g, d, (y + 4 - d) % 4, here).wait_recv()
            contract(g)
            for d in range(1, 4):
                rs_copy(g, d).start()
        if 1 <= g <= 4:
            y_start(g - 1)
        if 2 <= g:
            final_start(g - 2)

    for b in range(NB):
        for j in range(2):
            for yy in range(4):
                remote(
                    fsend.at[0], out.at[b, j, pl.ds(yy * QR, QR)], fssend.at[0, 0],
                    fsrecv.at[b * 8 + j * 4 + yy], here,
                ).wait_recv()

    for d in range(4):
        for b in range(NB):
            finish_send(f1_copies(b, d))
    for h in range(NCH):
        for g in range(len(groups(h))):
            for copy in gather_copies(h, g)[0]:
                copy.wait_send()
    for g in range(4):
        for d in range(1, 4):
            f2_copy(g, d, y, here).wait_send()
            rs_copy(g, d).wait_send()
            y_copy(g, d).wait_send()
        for d in range(4):
            finish_send(final_copies(g, d))


def per_device(integrals, coefficients, owned_tiles, pair_list, amplitudes):
    q_rows, occ, ao = integrals.shape
    nv = coefficients.shape[1]
    dma = pltpu.SemaphoreType.DMA
    vmem = pl.BlockSpec(memory_space=pltpu.VMEM)
    smem = pl.BlockSpec(memory_space=pltpu.SMEM)
    hbm = pl.BlockSpec(memory_space=pl.ANY)
    return pl.pallas_call(
        functools.partial(kernel, q_rows),
        out_shape=jax.ShapeDtypeStruct((NB, 2, T, T), F32),
        in_specs=[smem, smem, hbm, hbm, vmem],
        out_specs=vmem,
        scratch_shapes=[
            pltpu.VMEM((NCH, CH * NOCC, ao), BF16),
            pltpu.VMEM((nv // CB, ao, CB), BF16),
            pltpu.VMEM((CB // T, CH * NOCC, T), F32),
            pltpu.VMEM((NB, NT, CH, T), BF16),
            pltpu.VMEM((NCH, NB, NT + 4, CH, T), BF16),
            pltpu.VMEM((NCH, WIN, NSRC * CH, T), BF16),
            pltpu.VMEM((BLK // 2, 2 * T, 6 * T), F32),
            pltpu.VMEM((NB, 2, NOFF, T, T), BF16),
            pltpu.VMEM((BLK, NOFF, T, T), BF16),
            pltpu.VMEM((BLK, T, T), F32),
            pltpu.VMEM((4, 3, T, T), F32),
            pltpu.VMEM((4, T, T), F32),
            pltpu.VMEM((4, 3, QR, T), F32),
            pltpu.VMEM((4, QR, T), F32),
            dma((NCH,)),
            dma((nv // CB,)),
            dma((NCH + 3, 7)),
            dma((NCH + 3, NSRC)),
            dma((NB, 4)),
            dma((NSRC,)),
            dma((4, 3)),
            dma((4, 3)),
            dma((4, 3)),
            dma((4, 3)),
            dma((4, 3)),
            dma((4, 3)),
            dma((4, 4)),
            dma((16,)),
            dma((NCH + 3,)),
        ],
        compiler_params=pltpu.CompilerParams(
            collective_id=0, has_side_effects=True, vmem_limit_bytes=60 * 2**20
        ),
        name="residual_kernel",
    )(
        owned_tiles,
        pair_list,
        integrals.reshape(q_rows * occ, ao),
        coefficients,
        amplitudes,
    )


def solution(mesh):
    in_specs = (
        P(("aux", "tile"), None, None),
        P(),
        P(),
        P(None, "tile", None),
        P(None, "tile", None, None, None),
    )
    out_specs = P(None, "tile", None, None)
    return jax.shard_map(
        per_device, mesh=mesh, in_specs=in_specs, out_specs=out_specs, check_vma=False
    )
```

```python
import functools

import jax
import jax.numpy as jnp
from jax import lax
from jax.experimental import pallas as pl
from jax.experimental.pallas import tpu as pltpu
from jax.sharding import PartitionSpec as P

MESH = pl.DeviceIdType.MESH
F32 = jnp.float32
BF16 = jnp.bfloat16

NB = 2
T = 128
NT = 64
NOCC = 8
NOFF = 5
BLK = 16
WIN = BLK + 4
CHUNKS = (32, 32, 32)
START = (0, 32, 64)
NCH = len(CHUNKS)
ROWS = sum(CHUNKS)
NSRC = 8
CB = 256
QR = T // 4


def dev(x, y, z, c):
    return (y, x * 8 + z * 2 + c)


def remote(src, dst, ssem, rsem, where):
    return pltpu.make_async_remote_copy(
        src_ref=src, dst_ref=dst, send_sem=ssem, recv_sem=rsem, device_id=where, device_id_type=MESH
    )


def kernel(
    q_rows,
    owned, plist, integ, coef, amp, out,
    lhs, cbuf, acc, ynat, send, recv, rr, offs, offbuf, amp5, ampbuf, res, rsgot, ysend, ygot, fsend,
    lsem, csem, gsend, grecv, f1send, f1recv, f2send, f2recv, rssend, rsrecv, yssend, ysrecv,
    fssend, fsrecv, locsem,
):
    y = lax.axis_index("aux")
    t = lax.axis_index("tile")
    x = t // 8
    z = (t // 2) % 4
    c = t % 2
    l = x * (1 - c) + z * c
    o = z * (1 - c) + x * c
    here = dev(x, y, z, c)
    nblk = coef.shape[1] // CB
    tail = q_rows - START[-1]

    def lhs_copy(h):
        part = pl.ds(START[h] * NOCC, (CHUNKS[h] if h < NCH - 1 else tail) * NOCC)
        return pltpu.make_async_copy(integ.at[part], lhs.at[part], lsem.at[h])

    def coef_copy(n):
        return pltpu.make_async_copy(
            coef.at[:, pl.ds(pl.multiple_of(n * CB, CB), CB)], cbuf.at[n], csem.at[n]
        )

    lhs_copy(0).start()
    for n in range(nblk):
        coef_copy(n).start()
    for h in range(1, NCH):
        lhs_copy(h).start()

    bar = pltpu.get_barrier_semaphore()

    def greet(where):
        pl.semaphore_signal(bar, inc=1, device_id=where, device_id_type=MESH)

    def greet_sources(k, carry):
        p, cc = k // 2, k % 2
        greet(dev(x * c + p * (1 - c), y, z * (1 - c) + p * c, cc))
        greet(dev(l, y, p, cc))
        return carry

    lax.fori_loop(0, 8, greet_sources, 0)
    for d in range(1, 4):
        greet(dev((x + d * c) % 4, y, (z + d * (1 - c)) % 4, c))
        greet(dev(x, (y + d) % 4, z, c))

    for b in range(NB):
        for j in range(2):
            for k in range(4):
                p = plist[b, j, k]
                off = jnp.where(p >= 0, p - (2 * t + j) + 2, -1).astype(F32)
                offs[b, pl.ds(4 * j + k, 1)] = jnp.full((1, T), off, F32)

    def start_either(copies):
        far, near, is_self = copies
        if is_self is None:
            far.start()
        else:

            @pl.when(is_self)
            def _():
                near.start()

            @pl.when(jnp.logical_not(is_self))
            def _():
                far.start()

    def finish_send(copies):
        far, near, is_self = copies
        if is_self is None:
            far.wait_send()
        else:

            @pl.when(jnp.logical_not(is_self))
            def _():
                far.wait_send()

    def quarter_of(yy):
        return pl.ds(pl.multiple_of(yy * QR, QR), QR)

    quarter = quarter_of(y)
    me8 = z * 2 + c

    def f1_copies(b, d):
        src = amp.at[b, :, :, quarter]
        dst = ampbuf.at[pl.ds(me8 * 2, 2), :, quarter]
        if b == 0:
            where, is_self = dev(x, y, (z + d) % 4, 0), c == 0
        else:
            where, is_self = dev((x + d) % 4, y, x, 1), (c == 1) & (z == x)
        is_self = is_self if d == 0 else None
        far = remote(src, dst, f1send.at[0, b, d], f1recv.at[0, me8], where)
        near = pltpu.make_async_copy(src, dst, f1recv.at[0, me8])
        far_offs = remote(
            offs.at[b], offbuf.at[me8], f1send.at[1, b, d], f1recv.at[1, me8], where
        )
        near_offs = pltpu.make_async_copy(offs.at[b], offbuf.at[me8], f1recv.at[1, me8])
        return (far_offs, near_offs, is_self), (far, near, is_self)

    def f2_copy(g, d, yy, where):
        part = ampbuf.at[pl.ds(4 * g, 4), :, quarter_of(yy)]
        return remote(part, part, f2send.at[g, d - 1], f2recv.at[g, d - 1], where)

    def f2_start(g):
        for k in (2 * g, 2 * g + 1):
            remote(
                offs.at[0], offbuf.at[k], f1send.at[1, 0, 0], f1recv.at[1, k], here
            ).wait_recv()
            remote(
                amp.at[0, :, :, quarter], ampbuf.at[pl.ds(2 * k, 2), :, quarter],
                f1send.at[0, 0, 0], f1recv.at[0, k], here,
            ).wait_recv()
        for d in range(1, 4):
            f2_copy(g, d, y, dev(x, (y + d) % 4, z, c)).start()

    def f2_wait(g):
        for d in range(1, 4):
            f2_copy(g, d, (y + 4 - d) % 4, here).wait_recv()

    def by_offset(g):
        for e in range(4):
            k8, r = 2 * g + e // 2, 4 * (e % 2)
            for m in range(NOFF):
                total = None
                for k in range(4):
                    row = offbuf[k8, pl.ds(r + k, 1)]
                    hit = jnp.where(row == float(m), 1.0, 0.0).astype(BF16)
                    term = jnp.broadcast_to(hit, (T, T)) * ampbuf[4 * g + e, k]
                    total = term if total is None else total + term
                amp5[4 * g + e, pl.ds(m * T, T)] = total

    def half(h, n):
        rows_h = CHUNKS[h]
        mine = lhs[pl.ds(START[h] * NOCC, rows_h * NOCC)]
        whole = jnp.dot(mine, cbuf[n], preferred_element_type=F32)
        for a in range(CB // T):
            acc[a, pl.ds(0, rows_h * NOCC)] = whole[:, a * T : (a + 1) * T]
        for i in range(NOCC):
            for a in range(CB // T):
                part = acc[a, pl.ds(i, rows_h, stride=NOCC), :]
                if h == NCH - 1:
                    rows = lax.broadcasted_iota(jnp.int32, (rows_h, T), 0)
                    part = jnp.where(rows < tail, part, 0.0)
                ynat[i // 4, (i % 4) * 16 + 2 * n + a, pl.ds(0, rows_h)] = part.astype(BF16)

    def reorder(h):
        for b in range(NB):

            def one(s, carry):
                send[b, s, pl.ds(START[h], CHUNKS[h])] = ynat[
                    b, owned[b, (s + NT - 2) % NT], pl.ds(0, CHUNKS[h])
                ]
                return carry

            lax.fori_loop(0, NT + 4, one, 0, unroll=4)

    def place(h, k):
        rows_h = CHUNKS[h]
        return pl.ds(pl.multiple_of(START[h] * NSRC + k * rows_h, 16), rows_h)

    def part(h):
        return pl.ds(START[h], CHUNKS[h])

    def groups(h):
        return ((0, 8), (8, 4), (12, 4), (16, 4)) if h == NCH - 1 else ((0, WIN),)

    def gather_copies(h, g):
        low, count = groups(h)[g]
        q = h + g
        copies = []
        for d in range(1, 4):
            xd, zd = (x + d) % 4, (z + d) % 4
            for b, at, k, where in (
                (0, xd, x * 2 + c, dev(xd, y, z, 0)),
                (1, zd, z * 2 + c, dev(x, y, zd, 1)),
            ):
                copies.append(
                    remote(
                        send.at[b, pl.ds(at * BLK + low, count), part(h)],
                        recv.at[pl.ds(low, count), place(h, k)],
                        gsend.at[q, len(copies)],
                        grecv.at[q, k],
                        where,
                    )
                )
        copies.append(
            remote(
                send.at[1 - c, pl.ds(o * BLK + low, count), part(h)],
                recv.at[pl.ds(low, count), place(h, o * 2 + c)],
                gsend.at[q, 6],
                grecv.at[q, o * 2 + c],
                dev(x, y, z, 1 - c),
            )
        )
        own = pltpu.make_async_copy(
            send.at[c, pl.ds(l * BLK + low, count), part(h)],
            recv.at[pl.ds(low, count), place(h, l * 2 + c)],
            locsem.at[q],
        )
        return copies, own

    def gather_start(h):
        for g in range(len(groups(h))):
            copies, own = gather_copies(h, g)
            for copy in copies:
                copy.start()
            own.start()

    def gather_wait(h, g):
        low, count = groups(h)[g]
        q = h + g
        gather_copies(h, g)[1].wait()

        def arrived(k):
            remote(
                send.at[0, pl.ds(low, count), part(h)], recv.at[pl.ds(low, count), place(h, k)],
                gsend.at[q, 0], grecv.at[q, k], here,
            ).wait_recv()

        arrived(l * 2 + 1 - c)
        for d in range(1, 4):
            for cc in range(2):
                arrived(((l + d) % 4) * 2 + cc)

    def pairs(low, high, first, last):
        rows = pl.ds(low * NSRC, (high - low) * NSRC)

        def one(j, carry):
            mine = jnp.concatenate([recv[2 * j + 2, rows], recv[2 * j + 3, rows]], axis=1)
            others = jnp.concatenate([recv[2 * j + m, rows] for m in range(6)], axis=1)
            got = lax.dot_general(
                mine, others, (((0,), (0,)), ((), ())), preferred_element_type=F32
            )
            if low == 0:
                rr[j] = got
            else:
                rr[j] = rr[j] + got
            return carry

        lax.fori_loop(first, last, one, 0)

    def contract(g):
        for e in range(4):
            j, u = 2 * g + e // 2, e % 2
            whole = rr[j, pl.ds(u * T, T), pl.ds(u * T, NOFF * T)]
            high = whole.astype(BF16)
            low = (whole - high.astype(F32)).astype(BF16)
            weights = amp5[4 * g + e]
            res[4 * g + e] = jnp.dot(high, weights, preferred_element_type=F32) + jnp.dot(
                low, weights, preferred_element_type=F32
            )

    def rs_copy(g, d):
        return remote(
            res.at[4 * g + (o + d) % 4], rsgot.at[g, d - 1], rssend.at[g, d - 1], rsrecv.at[g, d - 1],
            dev((x + d * c) % 4, y, (z + d * (1 - c)) % 4, c),
        )

    def y_copy(g, d):
        return remote(
            ysend.at[g, quarter_of((y + d) % 4)], ygot.at[g, d - 1], yssend.at[g, d - 1],
            ysrecv.at[g, d - 1], dev(x, (y + d) % 4, z, c),
        )

    def y_start(g):
        for d in range(1, 4):
            rs_copy(g, d).wait_recv()
        ysend[g] = (res[4 * g + o] + rsgot[g, 0]) + (rsgot[g, 1] + rsgot[g, 2])
        for d in range(1, 4):
            y_copy(g, d).start()

    def final_copies(g, d):
        dst = out.at[c, o % 2, quarter]
        sem = fsrecv.at[c * 8 + (o % 2) * 4 + y]
        far = remote(fsend.at[g], dst, fssend.at[g, d], sem, dev(l, (y + d) % 4, g, o // 2))
        near = pltpu.make_async_copy(fsend.at[g], dst, sem)
        is_self = ((o // 2 == c) & (l == x) & (z == g)) if d == 0 else None
        return far, near, is_self

    def final_start(g):
        for d in range(1, 4):
            y_copy(g, d).wait_recv()
        fsend[g] = (ysend[g, quarter] + ygot[g, 0]) + (ygot[g, 1] + ygot[g, 2])
        for d in range(4):
            start_either(final_copies(g, d))

    def block(h):
        def one(n, carry):
            if h == 0:
                coef_copy(n).wait()
            half(h, n)
            return carry

        return one

    lhs_copy(0).wait()
    lax.fori_loop(0, 1, block(0), 0)
    pl.semaphore_wait(bar, 22)
    for d in range(4):
        for b in range(NB):
            for one in f1_copies(b, d):
                start_either(one)
    lax.fori_loop(1, nblk, block(0), 0)
    reorder(0)
    gather_start(0)
    lhs_copy(1).wait()
    lax.fori_loop(0, nblk // 2, block(1), 0)
    for g in range(4):
        f2_start(g)
    lax.fori_loop(nblk // 2, nblk, block(1), 0)
    reorder(1)
    gather_start(1)
    lhs_copy(2).wait()
    lax.fori_loop(0, nblk, block(2), 0)
    reorder(2)
    gather_start(2)
    for h in range(NCH - 1):
        gather_wait(h, 0)
    pairs(0, START[-1], 0, BLK // 2)
    for g in range(4):
        f2_wait(g)
        by_offset(g)
        gather_wait(NCH - 1, g)
        pairs(START[-1], ROWS, 2 * g, 2 * g + 2)
        contract(g)
        for d in range(1, 4):
            rs_copy(g, d).start()
    for g in range(4):
        y_start(g)
    for g in range(4):
        final_start(g)

    for b in range(NB):
        for j in range(2):
            for yy in range(4):
                remote(
                    fsend.at[0], out.at[b, j, pl.ds(yy * QR, QR)], fssend.at[0, 0],
                    fsrecv.at[b * 8 + j * 4 + yy], here,
                ).wait_recv()

    for d in range(4):
        for b in range(NB):
            for one in f1_copies(b, d):
                finish_send(one)
    for h in range(NCH):
        for g in range(len(groups(h))):
            for copy in gather_copies(h, g)[0]:
                copy.wait_send()
    for g in range(4):
        for d in range(1, 4):
            f2_copy(g, d, y, here).wait_send()
            rs_copy(g, d).wait_send()
            y_copy(g, d).wait_send()
        for d in range(4):
            finish_send(final_copies(g, d))


def per_device(integrals, coefficients, owned_tiles, pair_list, amplitudes):
    q_rows, occ, ao = integrals.shape
    nv = coefficients.shape[1]
    dma = pltpu.SemaphoreType.DMA
    vmem = pl.BlockSpec(memory_space=pltpu.VMEM)
    smem = pl.BlockSpec(memory_space=pltpu.SMEM)
    hbm = pl.BlockSpec(memory_space=pl.ANY)
    return pl.pallas_call(
        functools.partial(kernel, q_rows),
        out_shape=jax.ShapeDtypeStruct((NB, 2, T, T), F32),
        in_specs=[smem, smem, hbm, hbm, vmem],
        out_specs=vmem,
        scratch_shapes=[
            pltpu.VMEM((ROWS * NOCC, ao), BF16),
            pltpu.VMEM((nv // CB, ao, CB), BF16),
            pltpu.VMEM((CB // T, max(CHUNKS) * NOCC, T), F32),
            pltpu.VMEM((NB, NT, max(CHUNKS), T), BF16),
            pltpu.VMEM((NB, NT + 4, ROWS, T), BF16),
            pltpu.VMEM((WIN, NSRC * ROWS, T), BF16),
            pltpu.VMEM((BLK // 2, 2 * T, 6 * T), F32),
            pltpu.VMEM((NB, 8, T), F32),
            pltpu.VMEM((NSRC, 8, T), F32),
            pltpu.VMEM((BLK, NOFF * T, T), BF16),
            pltpu.VMEM((BLK, 4, T, T), BF16),
            pltpu.VMEM((BLK, T, T), F32),
            pltpu.VMEM((4, 3, T, T), F32),
            pltpu.VMEM((4, T, T), F32),
            pltpu.VMEM((4, 3, QR, T), F32),
            pltpu.VMEM((4, QR, T), F32),
            dma((NCH,)),
            dma((nv // CB,)),
            dma((NCH + 3, 7)),
            dma((NCH + 3, NSRC)),
            dma((2, NB, 4)),
            dma((2, NSRC)),
            dma((4, 3)),
            dma((4, 3)),
            dma((4, 3)),
            dma((4, 3)),
            dma((4, 3)),
            dma((4, 3)),
            dma((4, 4)),
            dma((16,)),
            dma((NCH + 3,)),
        ],
        compiler_params=pltpu.CompilerParams(
            collective_id=0, has_side_effects=True, vmem_limit_bytes=60 * 2**20
        ),
        name="residual_kernel",
    )(
        owned_tiles,
        pair_list,
        integrals.reshape(q_rows * occ, ao),
        coefficients,
        amplitudes,
    )


def solution(mesh):
    in_specs = (
        P(("aux", "tile"), None, None),
        P(),
        P(),
        P(None, "tile", None),
        P(None, "tile", None, None, None),
    )
    out_specs = P(None, "tile", None, None)
    return jax.shard_map(
        per_device, mesh=mesh, in_specs=in_specs, out_specs=out_specs, check_vma=False
    )
```

```python
import functools

import jax
import jax.numpy as jnp
from jax import lax
from jax.experimental import pallas as pl
from jax.experimental.pallas import tpu as pltpu
from jax.sharding import PartitionSpec as P

MESH = pl.DeviceIdType.MESH
F32 = jnp.float32
BF16 = jnp.bfloat16

NB = 2
T = 128
NT = 64
NOCC = 8
NOFF = 5
BLK = 16
WIN = BLK + 4
CHUNKS = (32, 32, 32)
START = (0, 32, 64)
NCH = len(CHUNKS)
ROWS = sum(CHUNKS)
NSRC = 8
CB = 256
QR = T // 4
Y_FIRST = (False, False, False, False)


def dev(x, y, z, c):
    return (y, x * 8 + z * 2 + c)


def remote(src, dst, ssem, rsem, where):
    return pltpu.make_async_remote_copy(
        src_ref=src, dst_ref=dst, send_sem=ssem, recv_sem=rsem, device_id=where, device_id_type=MESH
    )


def kernel(
    q_rows,
    owned, plist, integ, coef, amp, out,
    lhs, cbuf, acc, ynat, send, recv, rr, offs, offbuf, amp5, ampbuf, res, rsgot, ysend, ygot4, ysend4, ygot, fsend,
    lsem, csem, gsend, grecv, f1send, f1recv, f2send, f2recv, rssend, rsrecv, yssend, ysrecv,
    fssend, fsrecv, locsem,
):
    y = lax.axis_index("aux")
    t = lax.axis_index("tile")
    x = t // 8
    z = (t // 2) % 4
    c = t % 2
    l = x * (1 - c) + z * c
    o = z * (1 - c) + x * c
    here = dev(x, y, z, c)
    nblk = coef.shape[1] // CB
    tail = q_rows - START[-1]

    def lhs_copy(h):
        part = pl.ds(START[h] * NOCC, (CHUNKS[h] if h < NCH - 1 else tail) * NOCC)
        return pltpu.make_async_copy(integ.at[part], lhs.at[part], lsem.at[h])

    def coef_copy(n):
        return pltpu.make_async_copy(
            coef.at[:, pl.ds(pl.multiple_of(n * CB, CB), CB)], cbuf.at[n], csem.at[n]
        )

    lhs_copy(0).start()
    for n in range(nblk):
        coef_copy(n).start()
    for h in range(1, NCH):
        lhs_copy(h).start()

    bar = pltpu.get_barrier_semaphore()

    def greet(where):
        pl.semaphore_signal(bar, inc=1, device_id=where, device_id_type=MESH)

    def greet_sources(k, carry):
        p, cc = k // 2, k % 2
        greet(dev(x * c + p * (1 - c), y, z * (1 - c) + p * c, cc))
        greet(dev(l, y, p, cc))
        return carry

    lax.fori_loop(0, 8, greet_sources, 0)
    for d in range(1, 4):
        greet(dev((x + d * c) % 4, y, (z + d * (1 - c)) % 4, c))
        greet(dev(x, (y + d) % 4, z, c))

    for b in range(NB):
        for j in range(2):
            for k in range(4):
                p = plist[b, j, k]
                off = jnp.where(p >= 0, p - (2 * t + j) + 2, -1).astype(F32)
                offs[b, pl.ds(4 * j + k, 1)] = jnp.full((1, T), off, F32)

    def start_either(copies):
        far, near, is_self = copies
        if is_self is None:
            far.start()
        else:

            @pl.when(is_self)
            def _():
                near.start()

            @pl.when(jnp.logical_not(is_self))
            def _():
                far.start()

    def finish_send(copies):
        far, near, is_self = copies
        if is_self is None:
            far.wait_send()
        else:

            @pl.when(jnp.logical_not(is_self))
            def _():
                far.wait_send()

    def quarter_of(yy):
        return pl.ds(pl.multiple_of(yy * QR, QR), QR)

    quarter = quarter_of(y)
    me8 = z * 2 + c

    def f1_copies(b, d):
        src = amp.at[b, :, :, quarter]
        dst = ampbuf.at[pl.ds(me8 * 2, 2), :, quarter]
        if b == 0:
            where, is_self = dev(x, y, (z + d) % 4, 0), c == 0
        else:
            where, is_self = dev((x + d) % 4, y, x, 1), (c == 1) & (z == x)
        is_self = is_self if d == 0 else None
        far = remote(src, dst, f1send.at[0, b, d], f1recv.at[0, me8], where)
        near = pltpu.make_async_copy(src, dst, f1recv.at[0, me8])
        far_offs = remote(
            offs.at[b], offbuf.at[me8], f1send.at[1, b, d], f1recv.at[1, me8], where
        )
        near_offs = pltpu.make_async_copy(offs.at[b], offbuf.at[me8], f1recv.at[1, me8])
        return (far_offs, near_offs, is_self), (far, near, is_self)

    def f2_copy(g, kind, receive=False):
        way = 1 - 2 * (kind % 2)
        back = (kind // 2 + (1 if receive else 0)) * way
        slots = pl.ds(4 * g, 4) if kind < 2 else pl.ds(4 * g + 2 * (kind - 2), 2)
        part = ampbuf.at[slots, :, quarter_of((y + 4 - back) % 4)]
        where = here if receive else dev(x, (y + 4 + way) % 4, z, c)
        return remote(part, part, f2send.at[g, kind], f2recv.at[g, kind], where)

    def f2_start(g):
        for k in (2 * g, 2 * g + 1):
            remote(
                offs.at[0], offbuf.at[k], f1send.at[1, 0, 0], f1recv.at[1, k], here
            ).wait_recv()
            remote(
                amp.at[0, :, :, quarter], ampbuf.at[pl.ds(2 * k, 2), :, quarter],
                f1send.at[0, 0, 0], f1recv.at[0, k], here,
            ).wait_recv()
        for kind in range(2):
            f2_copy(g, kind).start()

    def f2_forward(g):
        for kind in range(2):
            f2_copy(g, kind, receive=True).wait_recv()
        for kind in range(2, 4):
            f2_copy(g, kind).start()

    def f2_wait(g):
        for kind in range(2, 4):
            f2_copy(g, kind, receive=True).wait_recv()

    def by_offset(g):
        for e in range(4):
            k8, r = 2 * g + e // 2, 4 * (e % 2)
            for m in range(NOFF):
                total = None
                for k in range(4):
                    row = jnp.broadcast_to(offbuf[k8, pl.ds(r + k, 1)], (16, T))
                    hit = jnp.where(row == float(m), 1.0, 0.0).astype(BF16)
                    term = hit[None] * ampbuf[4 * g + e, k].reshape(T // 16, 16, T)
                    total = term if total is None else total + term
                amp5[4 * g + e, pl.ds(m * T, T)] = total.reshape(T, T)

    def half(h, n):
        rows_h = CHUNKS[h]
        mine = lhs[pl.ds(START[h] * NOCC, rows_h * NOCC)]
        whole = jnp.dot(mine, cbuf[n], preferred_element_type=F32)
        for a in range(CB // T):
            acc[a, pl.ds(0, rows_h * NOCC)] = whole[:, a * T : (a + 1) * T]
        for i in range(NOCC):
            for a in range(CB // T):
                part = acc[a, pl.ds(i, rows_h, stride=NOCC), :]
                if h == NCH - 1:
                    rows = lax.broadcasted_iota(jnp.int32, (rows_h, T), 0)
                    part = jnp.where(rows < tail, part, 0.0)
                ynat[i // 4, (i % 4) * 16 + 2 * n + a, pl.ds(0, rows_h)] = part.astype(BF16)

    def reorder(h):
        for b in range(NB):

            def one(s, carry):
                send[b, s, pl.ds(START[h], CHUNKS[h])] = ynat[
                    b, owned[b, (s + NT - 2) % NT], pl.ds(0, CHUNKS[h])
                ]
                return carry

            lax.fori_loop(0, NT + 4, one, 0, unroll=4)

    def place(h, k):
        rows_h = CHUNKS[h]
        return pl.ds(pl.multiple_of(START[h] * NSRC + k * rows_h, 16), rows_h)

    def part(h):
        return pl.ds(START[h], CHUNKS[h])

    def groups(h):
        return ((0, 8), (8, 4), (12, 4), (16, 4)) if h == NCH - 1 else ((0, WIN),)

    def gather_copies(h, g):
        low, count = groups(h)[g]
        q = h + g
        copies = []
        for d in range(1, 4):
            xd, zd = (x + d) % 4, (z + d) % 4
            for b, at, k, where in (
                (0, xd, x * 2 + c, dev(xd, y, z, 0)),
                (1, zd, z * 2 + c, dev(x, y, zd, 1)),
            ):
                copies.append(
                    remote(
                        send.at[b, pl.ds(at * BLK + low, count), part(h)],
                        recv.at[pl.ds(low, count), place(h, k)],
                        gsend.at[q, len(copies)],
                        grecv.at[q, k],
                        where,
                    )
                )
        copies.append(
            remote(
                send.at[1 - c, pl.ds(o * BLK + low, count), part(h)],
                recv.at[pl.ds(low, count), place(h, o * 2 + c)],
                gsend.at[q, 6],
                grecv.at[q, o * 2 + c],
                dev(x, y, z, 1 - c),
            )
        )
        own = pltpu.make_async_copy(
            send.at[c, pl.ds(l * BLK + low, count), part(h)],
            recv.at[pl.ds(low, count), place(h, l * 2 + c)],
            locsem.at[q],
        )
        return copies, own

    def gather_start(h):
        for g in range(len(groups(h))):
            copies, own = gather_copies(h, g)
            for copy in copies:
                copy.start()
            own.start()

    def gather_wait(h, g):
        low, count = groups(h)[g]
        q = h + g
        gather_copies(h, g)[1].wait()

        def arrived(k):
            remote(
                send.at[0, pl.ds(low, count), part(h)], recv.at[pl.ds(low, count), place(h, k)],
                gsend.at[q, 0], grecv.at[q, k], here,
            ).wait_recv()

        arrived(l * 2 + 1 - c)
        for d in range(1, 4):
            for cc in range(2):
                arrived(((l + d) % 4) * 2 + cc)

    def pairs(low, high, first, last):
        rows = pl.ds(low * NSRC, (high - low) * NSRC)

        def one(j, carry):
            mine = jnp.concatenate([recv[2 * j + 2, rows], recv[2 * j + 3, rows]], axis=1)
            others = jnp.concatenate([recv[2 * j + m, rows] for m in range(6)], axis=1)
            got = lax.dot_general(
                mine, others, (((0,), (0,)), ((), ())), preferred_element_type=F32
            )
            if low == 0:
                rr[j] = got
            else:
                rr[j] = rr[j] + got
            return carry

        lax.fori_loop(first, last, one, 0)

    def contract(g):
        for e in range(4):
            j, u = 2 * g + e // 2, e % 2
            whole = rr[j, pl.ds(u * T, T), pl.ds(u * T, NOFF * T)]
            high = whole.astype(BF16)
            low = (whole - high.astype(F32)).astype(BF16)
            weights = amp5[4 * g + e]
            res[4 * g + e] = jnp.dot(high, weights, preferred_element_type=F32) + jnp.dot(
                low, weights, preferred_element_type=F32
            )

    def first_copy(g, d):
        if Y_FIRST[g]:
            src = res.at[pl.ds(4 * g, 4), quarter_of((y + d) % 4)]
            return remote(
                src, ygot4.at[g, d - 1], rssend.at[g, d - 1], rsrecv.at[g, d - 1],
                dev(x, (y + d) % 4, z, c),
            )
        return remote(
            res.at[4 * g + (o + d) % 4], rsgot.at[g, d - 1], rssend.at[g, d - 1], rsrecv.at[g, d - 1],
            dev((x + d * c) % 4, y, (z + d * (1 - c)) % 4, c),
        )

    def second_copy(g, d):
        if Y_FIRST[g]:
            return remote(
                ysend4.at[g, (o + d) % 4], ygot.at[g, d - 1], yssend.at[g, d - 1],
                ysrecv.at[g, d - 1], dev((x + d * c) % 4, y, (z + d * (1 - c)) % 4, c),
            )
        return remote(
            ysend.at[g, quarter_of((y + d) % 4)], ygot.at[g, d - 1], yssend.at[g, d - 1],
            ysrecv.at[g, d - 1], dev(x, (y + d) % 4, z, c),
        )

    def second_start(g):
        for d in range(1, 4):
            first_copy(g, d).wait_recv()
        if Y_FIRST[g]:
            ysend4[g] = (res[pl.ds(4 * g, 4), quarter] + ygot4[g, 0]) + (ygot4[g, 1] + ygot4[g, 2])
        else:
            ysend[g] = (res[4 * g + o] + rsgot[g, 0]) + (rsgot[g, 1] + rsgot[g, 2])
        for d in range(1, 4):
            second_copy(g, d).start()

    def final_copies(g, d):
        dst = out.at[c, o % 2, quarter]
        sem = fsrecv.at[c * 8 + (o % 2) * 4 + y]
        far = remote(fsend.at[g], dst, fssend.at[g, d], sem, dev(l, (y + d) % 4, g, o // 2))
        near = pltpu.make_async_copy(fsend.at[g], dst, sem)
        is_self = ((o // 2 == c) & (l == x) & (z == g)) if d == 0 else None
        return far, near, is_self

    def final_start(g):
        for d in range(1, 4):
            second_copy(g, d).wait_recv()
        mine = ysend4[g, o] if Y_FIRST[g] else ysend[g, quarter]
        fsend[g] = (mine + ygot[g, 0]) + (ygot[g, 1] + ygot[g, 2])
        for d in range(4):
            start_either(final_copies(g, d))

    def block(h):
        def one(n, carry):
            if h == 0:
                coef_copy(n).wait()
            half(h, n)
            return carry

        return one

    lhs_copy(0).wait()
    lax.fori_loop(0, 1, block(0), 0)
    pl.semaphore_wait(bar, 22)
    for d in range(4):
        for b in range(NB):
            for one in f1_copies(b, d):
                start_either(one)
    lax.fori_loop(1, nblk, block(0), 0)
    reorder(0)
    gather_start(0)
    lhs_copy(1).wait()
    lax.fori_loop(0, nblk // 2, block(1), 0)
    for g in range(4):
        f2_start(g)
    lax.fori_loop(nblk // 2, nblk, block(1), 0)
    reorder(1)
    gather_start(1)
    lhs_copy(2).wait()
    lax.fori_loop(0, nblk // 2, block(2), 0)
    f2_forward(0)
    lax.fori_loop(nblk // 2, nblk, block(2), 0)
    reorder(2)
    gather_start(2)
    f2_forward(1)
    gather_wait(0, 0)
    pairs(0, START[1], 0, BLK // 2)
    f2_forward(2)
    f2_forward(3)
    gather_wait(1, 0)
    pairs(START[1], START[2], 0, BLK // 2)
    for g in range(4):
        gather_wait(2, g)
        pairs(START[2], ROWS, 2 * g, 2 * g + 2)
        f2_wait(g)
        by_offset(g)
        contract(g)
        for d in range(1, 4):
            first_copy(g, d).start()
    for g in range(4):
        second_start(g)
    for g in range(4):
        final_start(g)

    for b in range(NB):
        for j in range(2):
            for yy in range(4):
                remote(
                    fsend.at[0], out.at[b, j, pl.ds(yy * QR, QR)], fssend.at[0, 0],
                    fsrecv.at[b * 8 + j * 4 + yy], here,
                ).wait_recv()

    for d in range(4):
        for b in range(NB):
            for one in f1_copies(b, d):
                finish_send(one)
    for h in range(NCH):
        for g in range(len(groups(h))):
            for copy in gather_copies(h, g)[0]:
                copy.wait_send()
    for g in range(4):
        for kind in range(4):
            f2_copy(g, kind).wait_send()
        for d in range(1, 4):
            first_copy(g, d).wait_send()
            second_copy(g, d).wait_send()
        for d in range(4):
            finish_send(final_copies(g, d))


def per_device(integrals, coefficients, owned_tiles, pair_list, amplitudes):
    q_rows, occ, ao = integrals.shape
    nv = coefficients.shape[1]
    dma = pltpu.SemaphoreType.DMA
    vmem = pl.BlockSpec(memory_space=pltpu.VMEM)
    smem = pl.BlockSpec(memory_space=pltpu.SMEM)
    hbm = pl.BlockSpec(memory_space=pl.ANY)
    return pl.pallas_call(
        functools.partial(kernel, q_rows),
        out_shape=jax.ShapeDtypeStruct((NB, 2, T, T), F32),
        in_specs=[smem, smem, hbm, hbm, hbm],
        out_specs=vmem,
        scratch_shapes=[
            pltpu.VMEM((ROWS * NOCC, ao), BF16),
            pltpu.VMEM((nv // CB, ao, CB), BF16),
            pltpu.VMEM((CB // T, max(CHUNKS) * NOCC, T), F32),
            pltpu.VMEM((NB, NT, max(CHUNKS), T), BF16),
            pltpu.VMEM((NB, NT + 4, ROWS, T), BF16),
            pltpu.VMEM((WIN, NSRC * ROWS, T), BF16),
            pltpu.VMEM((BLK // 2, 2 * T, 6 * T), F32),
            pltpu.VMEM((NB, 8, T), F32),
            pltpu.VMEM((NSRC, 8, T), F32),
            pltpu.VMEM((BLK, NOFF * T, T), BF16),
            pltpu.VMEM((BLK, 4, T, T), BF16),
            pltpu.VMEM((BLK, T, T), F32),
            pltpu.VMEM((4, 3, T, T), F32),
            pltpu.VMEM((4, T, T), F32),
            pltpu.VMEM((4, 3, 4, QR, T), F32),
            pltpu.VMEM((4, 4, QR, T), F32),
            pltpu.VMEM((4, 3, QR, T), F32),
            pltpu.VMEM((4, QR, T), F32),
            dma((NCH,)),
            dma((nv // CB,)),
            dma((NCH + 3, 7)),
            dma((NCH + 3, NSRC)),
            dma((2, NB, 4)),
            dma((2, NSRC)),
            dma((4, 4)),
            dma((4, 4)),
            dma((4, 3)),
            dma((4, 3)),
            dma((4, 3)),
            dma((4, 3)),
            dma((4, 4)),
            dma((16,)),
            dma((NCH + 3,)),
        ],
        compiler_params=pltpu.CompilerParams(
            collective_id=0, has_side_effects=True, vmem_limit_bytes=60 * 2**20
        ),
        name="residual_kernel",
    )(
        owned_tiles,
        pair_list,
        integrals.reshape(q_rows * occ, ao),
        coefficients,
        amplitudes,
    )


def solution(mesh):
    in_specs = (
        P(("aux", "tile"), None, None),
        P(),
        P(),
        P(None, "tile", None),
        P(None, "tile", None, None, None),
    )
    out_specs = P(None, "tile", None, None)
    return jax.shard_map(
        per_device, mesh=mesh, in_specs=in_specs, out_specs=out_specs, check_vma=False
    )
```

```python
import functools

import jax
import jax.numpy as jnp
from jax import lax
from jax.experimental import pallas as pl
from jax.experimental.pallas import tpu as pltpu
from jax.sharding import PartitionSpec as P

MESH = pl.DeviceIdType.MESH
F32 = jnp.float32
BF16 = jnp.bfloat16

NB = 2
T = 128
NT = 64
NOCC = 8
NOFF = 5
BLK = 16
WIN = BLK + 4
CHUNKS = (32, 32, 32)
START = (0, 32, 64)
NCH = len(CHUNKS)
ROWS = sum(CHUNKS)
NSRC = 8
CB = 256
QR = T // 4


def dev(x, y, z, c):
    return (y, x * 8 + z * 2 + c)


def remote(src, dst, ssem, rsem, where):
    return pltpu.make_async_remote_copy(
        src_ref=src, dst_ref=dst, send_sem=ssem, recv_sem=rsem, device_id=where, device_id_type=MESH
    )


def kernel(
    q_rows,
    owned, plist, integ, coef, amp, out,
    lhs, cbuf, acc, ynat, send, recv, rr, offs, offbuf, amp5, ampbuf, res, rsgot, ysend, ygot, fsend,
    lsem, csem, gsend, grecv, f1send, f1recv, f2send, f2recv, rssend, rsrecv, yssend, ysrecv,
    fssend, fsrecv, locsem,
):
    y = lax.axis_index("aux")
    t = lax.axis_index("tile")
    x = t // 8
    z = (t // 2) % 4
    c = t % 2
    l = x * (1 - c) + z * c
    o = z * (1 - c) + x * c
    here = dev(x, y, z, c)
    nblk = coef.shape[1] // CB
    tail = q_rows - START[-1]

    def lhs_copy(h):
        part = pl.ds(START[h] * NOCC, (CHUNKS[h] if h < NCH - 1 else tail) * NOCC)
        return pltpu.make_async_copy(integ.at[part], lhs.at[part], lsem.at[h])

    def coef_copy(n):
        return pltpu.make_async_copy(
            coef.at[:, pl.ds(pl.multiple_of(n * CB, CB), CB)], cbuf.at[n], csem.at[n]
        )

    lhs_copy(0).start()
    for n in range(nblk):
        coef_copy(n).start()
    for h in range(1, NCH):
        lhs_copy(h).start()

    bar = pltpu.get_barrier_semaphore()

    def greet(where):
        pl.semaphore_signal(bar, inc=1, device_id=where, device_id_type=MESH)

    def greet_sources(k, carry):
        p, cc = k // 2, k % 2
        greet(dev(x * c + p * (1 - c), y, z * (1 - c) + p * c, cc))
        greet(dev(l, y, p, cc))
        return carry

    lax.fori_loop(0, 8, greet_sources, 0)
    for d in range(1, 4):
        greet(dev((x + d * c) % 4, y, (z + d * (1 - c)) % 4, c))
        greet(dev(x, (y + d) % 4, z, c))

    for b in range(NB):
        for j in range(2):
            for k in range(4):
                p = plist[b, j, k]
                off = jnp.where(p >= 0, p - (2 * t + j) + 2, -1).astype(F32)
                offs[b, pl.ds(4 * j + k, 1)] = jnp.full((1, T), off, F32)

    def start_either(copies):
        far, near, is_self = copies
        if is_self is None:
            far.start()
        else:

            @pl.when(is_self)
            def _():
                near.start()

            @pl.when(jnp.logical_not(is_self))
            def _():
                far.start()

    def finish_send(copies):
        far, near, is_self = copies
        if is_self is None:
            far.wait_send()
        else:

            @pl.when(jnp.logical_not(is_self))
            def _():
                far.wait_send()

    def quarter_of(yy):
        return pl.ds(pl.multiple_of(yy * QR, QR), QR)

    quarter = quarter_of(y)
    me8 = z * 2 + c

    def f1_copies(b, d):
        src = amp.at[b, :, :, quarter]
        dst = ampbuf.at[pl.ds(me8 * 2, 2), :, quarter]
        if b == 0:
            where, is_self = dev(x, y, (z + d) % 4, 0), c == 0
        else:
            where, is_self = dev((x + d) % 4, y, x, 1), (c == 1) & (z == x)
        is_self = is_self if d == 0 else None
        far = remote(src, dst, f1send.at[0, b, d], f1recv.at[0, me8], where)
        near = pltpu.make_async_copy(src, dst, f1recv.at[0, me8])
        far_offs = remote(
            offs.at[b], offbuf.at[me8], f1send.at[1, b, d], f1recv.at[1, me8], where
        )
        near_offs = pltpu.make_async_copy(offs.at[b], offbuf.at[me8], f1recv.at[1, me8])
        return (far_offs, near_offs, is_self), (far, near, is_self)

    def f2_copy(g, kind, receive=False):
        way = 1 - 2 * (kind % 2)
        back = (kind // 2 + (1 if receive else 0)) * way
        slots = pl.ds(4 * g, 4) if kind < 2 else pl.ds(4 * g + 2 * (kind - 2), 2)
        part = ampbuf.at[slots, :, quarter_of((y + 4 - back) % 4)]
        where = here if receive else dev(x, (y + 4 + way) % 4, z, c)
        return remote(part, part, f2send.at[g, kind], f2recv.at[g, kind], where)

    def f2_start(g):
        for k in (2 * g, 2 * g + 1):
            remote(
                offs.at[0], offbuf.at[k], f1send.at[1, 0, 0], f1recv.at[1, k], here
            ).wait_recv()
            remote(
                amp.at[0, :, :, quarter], ampbuf.at[pl.ds(2 * k, 2), :, quarter],
                f1send.at[0, 0, 0], f1recv.at[0, k], here,
            ).wait_recv()
        for kind in range(2):
            f2_copy(g, kind).start()

    def f2_forward(g):
        for kind in range(2):
            f2_copy(g, kind, receive=True).wait_recv()
        for kind in range(2, 4):
            f2_copy(g, kind).start()

    def f2_wait(g):
        for kind in range(2, 4):
            f2_copy(g, kind, receive=True).wait_recv()

    def by_offset(g):
        for e in range(4):
            k8, r = 2 * g + e // 2, 4 * (e % 2)
            for m in range(NOFF):
                total = None
                for k in range(4):
                    row = jnp.broadcast_to(offbuf[k8, pl.ds(r + k, 1)], (16, T))
                    hit = jnp.where(row == float(m), 1.0, 0.0).astype(BF16)
                    term = hit[None] * ampbuf[4 * g + e, k].reshape(T // 16, 16, T)
                    total = term if total is None else total + term
                amp5[4 * g + e, pl.ds(m * T, T)] = total.reshape(T, T)

    def half(h, n):
        rows_h = CHUNKS[h]
        mine = lhs[pl.ds(START[h] * NOCC, rows_h * NOCC)]
        whole = jnp.dot(mine, cbuf[n], preferred_element_type=F32)
        for a in range(CB // T):
            acc[a, pl.ds(0, rows_h * NOCC)] = whole[:, a * T : (a + 1) * T]
        for i in range(NOCC):
            for a in range(CB // T):
                part = acc[a, pl.ds(i, rows_h, stride=NOCC), :]
                if h == NCH - 1:
                    rows = lax.broadcasted_iota(jnp.int32, (rows_h, T), 0)
                    part = jnp.where(rows < tail, part, 0.0)
                ynat[i // 4, (i % 4) * 16 + 2 * n + a, pl.ds(0, rows_h)] = part.astype(BF16)

    def reorder(h):
        for b in range(NB):

            def one(s, carry):
                send[b, s, pl.ds(START[h], CHUNKS[h])] = ynat[
                    b, owned[b, (s + NT - 2) % NT], pl.ds(0, CHUNKS[h])
                ]
                return carry

            lax.fori_loop(0, NT + 4, one, 0, unroll=4)

    def place(h, k):
        rows_h = CHUNKS[h]
        return pl.ds(pl.multiple_of(START[h] * NSRC + k * rows_h, 16), rows_h)

    def part(h):
        return pl.ds(START[h], CHUNKS[h])

    def groups(h):
        return ((0, 8), (8, 4), (12, 4), (16, 4)) if h == NCH - 1 else ((0, WIN),)

    def gather_copies(h, g):
        low, count = groups(h)[g]
        q = h + g
        copies = []
        for d in range(1, 4):
            xd, zd = (x + d) % 4, (z + d) % 4
            for b, at, k, where in (
                (0, xd, x * 2 + c, dev(xd, y, z, 0)),
                (1, zd, z * 2 + c, dev(x, y, zd, 1)),
            ):
                copies.append(
                    remote(
                        send.at[b, pl.ds(at * BLK + low, count), part(h)],
                        recv.at[pl.ds(low, count), place(h, k)],
                        gsend.at[q, len(copies)],
                        grecv.at[q, k],
                        where,
                    )
                )
        copies.append(
            remote(
                send.at[1 - c, pl.ds(o * BLK + low, count), part(h)],
                recv.at[pl.ds(low, count), place(h, o * 2 + c)],
                gsend.at[q, 6],
                grecv.at[q, o * 2 + c],
                dev(x, y, z, 1 - c),
            )
        )
        own = pltpu.make_async_copy(
            send.at[c, pl.ds(l * BLK + low, count), part(h)],
            recv.at[pl.ds(low, count), place(h, l * 2 + c)],
            locsem.at[q],
        )
        return copies, own

    def gather_start(h):
        for g in range(len(groups(h))):
            copies, own = gather_copies(h, g)
            for copy in copies:
                copy.start()
            own.start()

    def gather_wait(h, g):
        low, count = groups(h)[g]
        q = h + g
        gather_copies(h, g)[1].wait()

        def arrived(k):
            remote(
                send.at[0, pl.ds(low, count), part(h)], recv.at[pl.ds(low, count), place(h, k)],
                gsend.at[q, 0], grecv.at[q, k], here,
            ).wait_recv()

        arrived(l * 2 + 1 - c)
        for d in range(1, 4):
            for cc in range(2):
                arrived(((l + d) % 4) * 2 + cc)

    def pairs(low, high, first, last):
        rows = pl.ds(low * NSRC, (high - low) * NSRC)

        def one(j, carry):
            mine = jnp.concatenate([recv[2 * j + 2, rows], recv[2 * j + 3, rows]], axis=1)
            others = jnp.concatenate([recv[2 * j + m, rows] for m in range(6)], axis=1)
            got = lax.dot_general(
                mine, others, (((0,), (0,)), ((), ())), preferred_element_type=F32
            )
            if low == 0:
                rr[j] = got
            else:
                rr[j] = rr[j] + got
            return carry

        lax.fori_loop(first, last, one, 0)

    def contract(g):
        for e in range(4):
            j, u = 2 * g + e // 2, e % 2
            whole = rr[j, pl.ds(u * T, T), pl.ds(u * T, NOFF * T)]
            high = whole.astype(BF16)
            low = (whole - high.astype(F32)).astype(BF16)
            weights = amp5[4 * g + e]
            res[4 * g + e] = jnp.dot(high, weights, preferred_element_type=F32) + jnp.dot(
                low, weights, preferred_element_type=F32
            )

    def first_copy(g, d):
        return remote(
            res.at[4 * g + (o + d) % 4], rsgot.at[g, d - 1], rssend.at[g, d - 1], rsrecv.at[g, d - 1],
            dev((x + d * c) % 4, y, (z + d * (1 - c)) % 4, c),
        )

    def second_copy(g, d):
        return remote(
            ysend.at[g, quarter_of((y + d) % 4)], ygot.at[g, d - 1], yssend.at[g, d - 1],
            ysrecv.at[g, d - 1], dev(x, (y + d) % 4, z, c),
        )

    def second_start(g):
        for d in range(1, 4):
            first_copy(g, d).wait_recv()
        ysend[g] = (res[4 * g + o] + rsgot[g, 0]) + (rsgot[g, 1] + rsgot[g, 2])
        for d in range(1, 4):
            second_copy(g, d).start()

    def final_copies(g, d):
        dst = out.at[c, o % 2, quarter]
        sem = fsrecv.at[c * 8 + (o % 2) * 4 + y]
        far = remote(fsend.at[g], dst, fssend.at[g, d], sem, dev(l, (y + d) % 4, g, o // 2))
        near = pltpu.make_async_copy(fsend.at[g], dst, sem)
        is_self = ((o // 2 == c) & (l == x) & (z == g)) if d == 0 else None
        return far, near, is_self

    def final_start(g):
        for d in range(1, 4):
            second_copy(g, d).wait_recv()
        fsend[g] = (ysend[g, quarter] + ygot[g, 0]) + (ygot[g, 1] + ygot[g, 2])
        for d in range(4):
            start_either(final_copies(g, d))

    def block(h):
        def one(n, carry):
            if h == 0:
                coef_copy(n).wait()
            half(h, n)
            return carry

        return one

    lhs_copy(0).wait()
    lax.fori_loop(0, 1, block(0), 0)
    pl.semaphore_wait(bar, 22)
    for d in range(4):
        for b in range(NB):
            for one in f1_copies(b, d):
                start_either(one)
    lax.fori_loop(1, nblk, block(0), 0)
    reorder(0)
    gather_start(0)
    lhs_copy(1).wait()
    lax.fori_loop(0, nblk // 2, block(1), 0)
    for g in range(4):
        f2_start(g)
    lax.fori_loop(nblk // 2, nblk, block(1), 0)
    reorder(1)
    gather_start(1)
    lhs_copy(2).wait()
    lax.fori_loop(0, nblk // 2, block(2), 0)
    f2_forward(0)
    lax.fori_loop(nblk // 2, nblk, block(2), 0)
    reorder(2)
    gather_start(2)
    f2_forward(1)
    gather_wait(0, 0)
    pairs(0, START[1], 0, BLK // 2)
    f2_forward(2)
    f2_forward(3)
    gather_wait(1, 0)
    pairs(START[1], START[2], 0, BLK // 2)
    for g in range(4):
        f2_wait(g)
        by_offset(g)
        gather_wait(2, g)
        pairs(START[2], ROWS, 2 * g, 2 * g + 2)
        contract(g)
        for d in range(1, 4):
            first_copy(g, d).start()
    for g in range(4):
        second_start(g)
    for g in range(4):
        final_start(g)

    for b in range(NB):
        for j in range(2):
            for yy in range(4):
                remote(
                    fsend.at[0], out.at[b, j, pl.ds(yy * QR, QR)], fssend.at[0, 0],
                    fsrecv.at[b * 8 + j * 4 + yy], here,
                ).wait_recv()

    for d in range(4):
        for b in range(NB):
            for one in f1_copies(b, d):
                finish_send(one)
    for h in range(NCH):
        for g in range(len(groups(h))):
            for copy in gather_copies(h, g)[0]:
                copy.wait_send()
    for g in range(4):
        for kind in range(4):
            f2_copy(g, kind).wait_send()
        for d in range(1, 4):
            first_copy(g, d).wait_send()
            second_copy(g, d).wait_send()
        for d in range(4):
            finish_send(final_copies(g, d))


def per_device(integrals, coefficients, owned_tiles, pair_list, amplitudes):
    q_rows, occ, ao = integrals.shape
    nv = coefficients.shape[1]
    dma = pltpu.SemaphoreType.DMA
    vmem = pl.BlockSpec(memory_space=pltpu.VMEM)
    smem = pl.BlockSpec(memory_space=pltpu.SMEM)
    hbm = pl.BlockSpec(memory_space=pl.ANY)
    return pl.pallas_call(
        functools.partial(kernel, q_rows),
        out_shape=jax.ShapeDtypeStruct((NB, 2, T, T), F32),
        in_specs=[smem, smem, hbm, hbm, hbm],
        out_specs=vmem,
        scratch_shapes=[
            pltpu.VMEM((ROWS * NOCC, ao), BF16),
            pltpu.VMEM((nv // CB, ao, CB), BF16),
            pltpu.VMEM((CB // T, max(CHUNKS) * NOCC, T), F32),
            pltpu.VMEM((NB, NT, max(CHUNKS), T), BF16),
            pltpu.VMEM((NB, NT + 4, ROWS, T), BF16),
            pltpu.VMEM((WIN, NSRC * ROWS, T), BF16),
            pltpu.VMEM((BLK // 2, 2 * T, 6 * T), F32),
            pltpu.VMEM((NB, 8, T), F32),
            pltpu.VMEM((NSRC, 8, T), F32),
            pltpu.VMEM((BLK, NOFF * T, T), BF16),
            pltpu.VMEM((BLK, 4, T, T), BF16),
            pltpu.VMEM((BLK, T, T), F32),
            pltpu.VMEM((4, 3, T, T), F32),
            pltpu.VMEM((4, T, T), F32),
            pltpu.VMEM((4, 3, QR, T), F32),
            pltpu.VMEM((4, QR, T), F32),
            dma((NCH,)),
            dma((nv // CB,)),
            dma((NCH + 3, 7)),
            dma((NCH + 3, NSRC)),
            dma((2, NB, 4)),
            dma((2, NSRC)),
            dma((4, 4)),
            dma((4, 4)),
            dma((4, 3)),
            dma((4, 3)),
            dma((4, 3)),
            dma((4, 3)),
            dma((4, 4)),
            dma((16,)),
            dma((NCH + 3,)),
        ],
        compiler_params=pltpu.CompilerParams(
            collective_id=0, has_side_effects=True, vmem_limit_bytes=60 * 2**20
        ),
        name="residual_kernel",
    )(
        owned_tiles,
        pair_list,
        integrals.reshape(q_rows * occ, ao),
        coefficients,
        amplitudes,
    )


def solution(mesh):
    in_specs = (
        P(("aux", "tile"), None, None),
        P(),
        P(),
        P(None, "tile", None),
        P(None, "tile", None, None, None),
    )
    out_specs = P(None, "tile", None, None)
    return jax.shard_map(
        per_device, mesh=mesh, in_specs=in_specs, out_specs=out_specs, check_vma=False
    )
```

```python
import functools

import jax
import jax.numpy as jnp
from jax import lax
from jax.experimental import pallas as pl
from jax.experimental.pallas import tpu as pltpu
from jax.sharding import PartitionSpec as P

MESH = pl.DeviceIdType.MESH
F32 = jnp.float32
BF16 = jnp.bfloat16

NB = 2
T = 128
NT = 64
NOCC = 8
NOFF = 5
BLK = 16
WIN = BLK + 4
CHUNKS = (32, 32, 32)
START = (0, 32, 64)
NCH = len(CHUNKS)
ROWS = sum(CHUNKS)
NSRC = 8
CB = 256
QR = T // 4


def dev(x, y, z, c):
    return (y, x * 8 + z * 2 + c)


def remote(src, dst, ssem, rsem, where):
    return pltpu.make_async_remote_copy(
        src_ref=src, dst_ref=dst, send_sem=ssem, recv_sem=rsem, device_id=where, device_id_type=MESH
    )


def kernel(
    q_rows,
    owned, plist, integ, coef, amp, out,
    lhs, cbuf, acc, ynat, send, recv, rr, offs, offbuf, amp5, ampbuf, res, rsgot, ysend, ygot, fsend,
    lsem, csem, gsend, grecv, f1send, f1recv, f2send, f2recv, rssend, rsrecv, yssend, ysrecv,
    fssend, fsrecv, locsem,
):
    y = lax.axis_index("aux")
    t = lax.axis_index("tile")
    x = t // 8
    z = (t // 2) % 4
    c = t % 2
    l = x * (1 - c) + z * c
    o = z * (1 - c) + x * c
    here = dev(x, y, z, c)
    nblk = coef.shape[1] // CB
    tail = q_rows - START[-1]

    def lhs_copy(h):
        part = pl.ds(START[h] * NOCC, (CHUNKS[h] if h < NCH - 1 else tail) * NOCC)
        return pltpu.make_async_copy(integ.at[part], lhs.at[part], lsem.at[h])

    def coef_copy(n):
        return pltpu.make_async_copy(
            coef.at[:, pl.ds(pl.multiple_of(n * CB, CB), CB)], cbuf.at[n], csem.at[n]
        )

    lhs_copy(0).start()
    for n in range(nblk):
        coef_copy(n).start()
    for h in range(1, NCH):
        lhs_copy(h).start()

    bar = pltpu.get_barrier_semaphore()

    def greet(where):
        pl.semaphore_signal(bar, inc=1, device_id=where, device_id_type=MESH)

    def greet_sources(k, carry):
        p, cc = k // 2, k % 2
        greet(dev(x * c + p * (1 - c), y, z * (1 - c) + p * c, cc))
        greet(dev(l, y, p, cc))
        return carry

    lax.fori_loop(0, 8, greet_sources, 0)
    for d in range(1, 4):
        greet(dev((x + d * c) % 4, y, (z + d * (1 - c)) % 4, c))
        greet(dev(x, (y + d) % 4, z, c))

    for b in range(NB):
        for j in range(2):
            for k in range(4):
                p = plist[b, j, k]
                off = jnp.where(p >= 0, p - (2 * t + j) + 2, -1).astype(F32)
                offs[b, pl.ds(4 * j + k, 1)] = jnp.full((1, T), off, F32)

    def start_either(copies):
        far, near, is_self = copies
        if is_self is None:
            far.start()
        else:

            @pl.when(is_self)
            def _():
                near.start()

            @pl.when(jnp.logical_not(is_self))
            def _():
                far.start()

    def finish_send(copies):
        far, near, is_self = copies
        if is_self is None:
            far.wait_send()
        else:

            @pl.when(jnp.logical_not(is_self))
            def _():
                far.wait_send()

    def quarter_of(yy):
        return pl.ds(pl.multiple_of(yy * QR, QR), QR)

    quarter = quarter_of(y)
    me8 = z * 2 + c

    def f1_copies(b, d):
        src = amp.at[b, :, :, quarter]
        dst = ampbuf.at[pl.ds(me8 * 2, 2), :, quarter]
        if b == 0:
            where, is_self = dev(x, y, (z + d) % 4, 0), c == 0
        else:
            where, is_self = dev((x + d) % 4, y, x, 1), (c == 1) & (z == x)
        is_self = is_self if d == 0 else None
        far = remote(src, dst, f1send.at[0, b, d], f1recv.at[0, me8], where)
        near = pltpu.make_async_copy(src, dst, f1recv.at[0, me8])
        far_offs = remote(
            offs.at[b], offbuf.at[me8], f1send.at[1, b, d], f1recv.at[1, me8], where
        )
        near_offs = pltpu.make_async_copy(offs.at[b], offbuf.at[me8], f1recv.at[1, me8])
        return (far_offs, near_offs, is_self), (far, near, is_self)

    def f2_copy(g, kind, receive=False):
        way = 1 - 2 * (kind % 2)
        back = (kind // 2 + (1 if receive else 0)) * way
        slots = pl.ds(4 * g, 4) if kind < 2 else pl.ds(4 * g + 2 * (kind - 2), 2)
        part = ampbuf.at[slots, :, quarter_of((y + 4 - back) % 4)]
        where = here if receive else dev(x, (y + 4 + way) % 4, z, c)
        return remote(part, part, f2send.at[g, kind], f2recv.at[g, kind], where)

    def f2_start(g):
        for k in (2 * g, 2 * g + 1):
            remote(
                offs.at[0], offbuf.at[k], f1send.at[1, 0, 0], f1recv.at[1, k], here
            ).wait_recv()
            remote(
                amp.at[0, :, :, quarter], ampbuf.at[pl.ds(2 * k, 2), :, quarter],
                f1send.at[0, 0, 0], f1recv.at[0, k], here,
            ).wait_recv()
        for kind in range(2):
            f2_copy(g, kind).start()

    def f2_forward(g):
        for kind in range(2):
            f2_copy(g, kind, receive=True).wait_recv()
        for kind in range(2, 4):
            f2_copy(g, kind).start()

    def f2_wait(g):
        for kind in range(2, 4):
            f2_copy(g, kind, receive=True).wait_recv()

    def by_offset(g):
        for e in range(4):
            k8, r = 2 * g + e // 2, 4 * (e % 2)
            for m in range(NOFF):
                total = None
                for k in range(4):
                    row = jnp.broadcast_to(offbuf[k8, pl.ds(r + k, 1)], (16, T))
                    hit = jnp.where(row == float(m), 1.0, 0.0).astype(BF16)
                    term = hit[None] * ampbuf[4 * g + e, k].reshape(T // 16, 16, T)
                    total = term if total is None else total + term
                amp5[4 * g + e, pl.ds(m * T, T)] = total.reshape(T, T)

    def half(h, n):
        rows_h = CHUNKS[h]
        mine = lhs[pl.ds(START[h] * NOCC, rows_h * NOCC)]
        whole = jnp.dot(mine, cbuf[n], preferred_element_type=F32)
        for a in range(CB // T):
            acc[a, pl.ds(0, rows_h * NOCC)] = whole[:, a * T : (a + 1) * T]
        for i in range(NOCC):
            for a in range(CB // T):
                part = acc[a, pl.ds(i, rows_h, stride=NOCC), :]
                if h == NCH - 1:
                    rows = lax.broadcasted_iota(jnp.int32, (rows_h, T), 0)
                    part = jnp.where(rows < tail, part, 0.0)
                ynat[i // 4, (i % 4) * 16 + 2 * n + a, pl.ds(0, rows_h)] = part.astype(BF16)

    def reorder(h):
        for b in range(NB):

            def one(s, carry):
                send[b, s, pl.ds(START[h], CHUNKS[h])] = ynat[
                    b, owned[b, (s + NT - 2) % NT], pl.ds(0, CHUNKS[h])
                ]
                return carry

            lax.fori_loop(0, NT + 4, one, 0, unroll=4)

    def place(h, k):
        rows_h = CHUNKS[h]
        return pl.ds(pl.multiple_of(START[h] * NSRC + k * rows_h, 16), rows_h)

    def part(h):
        return pl.ds(START[h], CHUNKS[h])

    def groups(h):
        return ((0, 8), (8, 4), (12, 4), (16, 4)) if h == NCH - 1 else ((0, WIN),)

    def gather_copies(h, g):
        low, count = groups(h)[g]
        q = h + g
        copies = []
        for d in range(1, 4):
            xd, zd = (x + d) % 4, (z + d) % 4
            for b, at, k, where in (
                (0, xd, x * 2 + c, dev(xd, y, z, 0)),
                (1, zd, z * 2 + c, dev(x, y, zd, 1)),
            ):
                copies.append(
                    remote(
                        send.at[b, pl.ds(at * BLK + low, count), part(h)],
                        recv.at[pl.ds(low, count), place(h, k)],
                        gsend.at[q, len(copies)],
                        grecv.at[q, k],
                        where,
                    )
                )
        copies.append(
            remote(
                send.at[1 - c, pl.ds(o * BLK + low, count), part(h)],
                recv.at[pl.ds(low, count), place(h, o * 2 + c)],
                gsend.at[q, 6],
                grecv.at[q, o * 2 + c],
                dev(x, y, z, 1 - c),
            )
        )
        own = pltpu.make_async_copy(
            send.at[c, pl.ds(l * BLK + low, count), part(h)],
            recv.at[pl.ds(low, count), place(h, l * 2 + c)],
            locsem.at[q],
        )
        return copies, own

    def gather_start(h):
        for g in range(len(groups(h))):
            copies, own = gather_copies(h, g)
            for copy in copies:
                copy.start()
            own.start()

    def gather_wait(h, g):
        low, count = groups(h)[g]
        q = h + g
        gather_copies(h, g)[1].wait()

        def arrived(k):
            remote(
                send.at[0, pl.ds(low, count), part(h)], recv.at[pl.ds(low, count), place(h, k)],
                gsend.at[q, 0], grecv.at[q, k], here,
            ).wait_recv()

        arrived(l * 2 + 1 - c)
        for d in range(1, 4):
            for cc in range(2):
                arrived(((l + d) % 4) * 2 + cc)

    def pairs(low, high, first, last):
        rows = pl.ds(low * NSRC, (high - low) * NSRC)

        def one(j, carry):
            mine = jnp.concatenate([recv[2 * j + 2, rows], recv[2 * j + 3, rows]], axis=1)
            others = jnp.concatenate([recv[2 * j + m, rows] for m in range(6)], axis=1)
            got = lax.dot_general(
                mine, others, (((0,), (0,)), ((), ())), preferred_element_type=F32
            )
            if low == 0:
                rr[j] = got
            else:
                rr[j] = rr[j] + got
            return carry

        lax.fori_loop(first, last, one, 0)

    def contract(g):
        for e in range(4):
            j, u = 2 * g + e // 2, e % 2
            whole = rr[j, pl.ds(u * T, T), pl.ds(u * T, NOFF * T)]
            high = whole.astype(BF16)
            low = (whole - high.astype(F32)).astype(BF16)
            weights = amp5[4 * g + e]
            res[4 * g + e] = jnp.dot(high, weights, preferred_element_type=F32) + jnp.dot(
                low, weights, preferred_element_type=F32
            )

    def first_copy(g, d):
        return remote(
            res.at[4 * g + (o + d) % 4], rsgot.at[g, d - 1], rssend.at[g, d - 1], rsrecv.at[g, d - 1],
            dev((x + d * c) % 4, y, (z + d * (1 - c)) % 4, c),
        )

    def second_copy(g, d):
        return remote(
            ysend.at[g, quarter_of((y + d) % 4)], ygot.at[g, d - 1], yssend.at[g, d - 1],
            ysrecv.at[g, d - 1], dev(x, (y + d) % 4, z, c),
        )

    def second_start(g):
        for d in range(1, 4):
            first_copy(g, d).wait_recv()
        ysend[g] = (res[4 * g + o] + rsgot[g, 0]) + (rsgot[g, 1] + rsgot[g, 2])
        for d in range(1, 4):
            second_copy(g, d).start()

    def final_copies(g, d):
        dst = out.at[c, o % 2, quarter]
        sem = fsrecv.at[c * 8 + (o % 2) * 4 + y]
        far = remote(fsend.at[g], dst, fssend.at[g, d], sem, dev(l, (y + d) % 4, g, o // 2))
        near = pltpu.make_async_copy(fsend.at[g], dst, sem)
        is_self = ((o // 2 == c) & (l == x) & (z == g)) if d == 0 else None
        return far, near, is_self

    def final_start(g):
        for d in range(1, 4):
            second_copy(g, d).wait_recv()
        fsend[g] = (ysend[g, quarter] + ygot[g, 0]) + (ygot[g, 1] + ygot[g, 2])
        for d in range(4):
            start_either(final_copies(g, d))

    def block(h):
        def one(n, carry):
            if h == 0:
                coef_copy(n).wait()
            half(h, n)
            return carry

        return one

    lhs_copy(0).wait()
    lax.fori_loop(0, 1, block(0), 0)
    pl.semaphore_wait(bar, 22)
    for d in range(4):
        for b in range(NB):
            for one in f1_copies(b, d):
                start_either(one)
    lax.fori_loop(1, nblk, block(0), 0)
    reorder(0)
    gather_start(0)
    lhs_copy(1).wait()
    lax.fori_loop(0, nblk // 2, block(1), 0)
    for g in range(4):
        f2_start(g)
    lax.fori_loop(nblk // 2, nblk, block(1), 0)
    reorder(1)
    gather_start(1)
    lhs_copy(2).wait()
    lax.fori_loop(0, nblk // 2, block(2), 0)
    f2_forward(0)
    lax.fori_loop(nblk // 2, nblk, block(2), 0)
    reorder(2)
    gather_start(2)
    f2_forward(1)
    gather_wait(0, 0)
    pairs(0, START[1], 0, BLK // 2)
    f2_forward(2)
    f2_forward(3)
    gather_wait(1, 0)
    pairs(START[1], START[2], 0, BLK // 2)
    for g in range(4):
        f2_wait(g)
        by_offset(g)
        gather_wait(2, g)
        pairs(START[2], ROWS, 2 * g, 2 * g + 2)
        contract(g)
        for d in range(1, 4):
            first_copy(g, d).start()
    for g in range(4):
        second_start(g)
    for g in range(4):
        final_start(g)

    for b in range(NB):
        for j in range(2):
            for yy in range(4):
                remote(
                    fsend.at[0], out.at[b, j, pl.ds(yy * QR, QR)], fssend.at[0, 0],
                    fsrecv.at[b * 8 + j * 4 + yy], here,
                ).wait_recv()

    for d in range(4):
        for b in range(NB):
            for one in f1_copies(b, d):
                finish_send(one)
    for h in range(NCH):
        for g in range(len(groups(h))):
            for copy in gather_copies(h, g)[0]:
                copy.wait_send()
    for g in range(4):
        for kind in range(4):
            f2_copy(g, kind).wait_send()
        for d in range(1, 4):
            first_copy(g, d).wait_send()
            second_copy(g, d).wait_send()
        for d in range(4):
            finish_send(final_copies(g, d))


def per_device(integrals, coefficients, owned_tiles, pair_list, amplitudes):
    q_rows, occ, ao = integrals.shape
    nv = coefficients.shape[1]
    dma = pltpu.SemaphoreType.DMA
    vmem = pl.BlockSpec(memory_space=pltpu.VMEM)
    smem = pl.BlockSpec(memory_space=pltpu.SMEM)
    hbm = pl.BlockSpec(memory_space=pl.ANY)
    return pl.pallas_call(
        functools.partial(kernel, q_rows),
        out_shape=jax.ShapeDtypeStruct((NB, 2, T, T), F32),
        in_specs=[smem, smem, hbm, hbm, hbm],
        out_specs=vmem,
        scratch_shapes=[
            pltpu.VMEM((ROWS * NOCC, ao), BF16),
            pltpu.VMEM((nv // CB, ao, CB), BF16),
            pltpu.VMEM((CB // T, (max(CHUNKS) + 1) * NOCC, T), F32),
            pltpu.VMEM((NB, NT, max(CHUNKS), T), BF16),
            pltpu.VMEM((NB, NT + 4, ROWS, T), BF16),
            pltpu.VMEM((WIN, NSRC * ROWS, T), BF16),
            pltpu.VMEM((BLK // 2, 2 * T, 6 * T), F32),
            pltpu.VMEM((NB, 8, T), F32),
            pltpu.VMEM((NSRC, 8, T), F32),
            pltpu.VMEM((BLK, NOFF * T, T), BF16),
            pltpu.VMEM((BLK, 4, T, T), BF16),
            pltpu.VMEM((BLK, T, T), F32),
            pltpu.VMEM((4, 3, T, T), F32),
            pltpu.VMEM((4, T, T), F32),
            pltpu.VMEM((4, 3, QR, T), F32),
            pltpu.VMEM((4, QR, T), F32),
            dma((NCH,)),
            dma((nv // CB,)),
            dma((NCH + 3, 7)),
            dma((NCH + 3, NSRC)),
            dma((2, NB, 4)),
            dma((2, NSRC)),
            dma((4, 4)),
            dma((4, 4)),
            dma((4, 3)),
            dma((4, 3)),
            dma((4, 3)),
            dma((4, 3)),
            dma((4, 4)),
            dma((16,)),
            dma((NCH + 3,)),
        ],
        compiler_params=pltpu.CompilerParams(
            collective_id=0, has_side_effects=True, vmem_limit_bytes=60 * 2**20
        ),
        name="residual_kernel",
    )(
        owned_tiles,
        pair_list,
        integrals.reshape(q_rows * occ, ao),
        coefficients,
        amplitudes,
    )


def solution(mesh):
    in_specs = (
        P(("aux", "tile"), None, None),
        P(),
        P(),
        P(None, "tile", None),
        P(None, "tile", None, None, None),
    )
    out_specs = P(None, "tile", None, None)
    return jax.shard_map(
        per_device, mesh=mesh, in_specs=in_specs, out_specs=out_specs, check_vma=False
    )
```

```python
import functools

import jax
import jax.numpy as jnp
from jax import lax
from jax.experimental import pallas as pl
from jax.experimental.pallas import tpu as pltpu
from jax.sharding import PartitionSpec as P

MESH = pl.DeviceIdType.MESH
F32 = jnp.float32
BF16 = jnp.bfloat16

NB = 2
T = 128
NT = 64
NOCC = 8
NOFF = 5
BLK = 16
WIN = BLK + 4
CHUNKS = (32, 32, 32)
START = (0, 32, 64)
NCH = len(CHUNKS)
ROWS = sum(CHUNKS)
NSRC = 8
CB = 256
QR = T // 4


def dev(x, y, z, c):
    return (y, x * 8 + z * 2 + c)


def remote(src, dst, ssem, rsem, where):
    return pltpu.make_async_remote_copy(
        src_ref=src, dst_ref=dst, send_sem=ssem, recv_sem=rsem, device_id=where, device_id_type=MESH
    )


def kernel(
    q_rows,
    owned, plist, integ, coef, amp, out,
    lhs, cbuf, acc, ynat, send, recv, rr, offs, offbuf, amp5, ampbuf, res, rsgot, ysend, ygot, fsend,
    lsem, csem, gsend, grecv, f1send, f1recv, f2send, f2recv, rssend, rsrecv, yssend, ysrecv,
    fssend, fsrecv, locsem,
):
    y = lax.axis_index("aux")
    t = lax.axis_index("tile")
    x = t // 8
    z = (t // 2) % 4
    c = t % 2
    l = x * (1 - c) + z * c
    o = z * (1 - c) + x * c
    here = dev(x, y, z, c)
    nblk = coef.shape[1] // CB
    tail = q_rows - START[-1]

    def lhs_copy(h):
        part = pl.ds(START[h] * NOCC, (CHUNKS[h] if h < NCH - 1 else tail) * NOCC)
        return pltpu.make_async_copy(integ.at[part], lhs.at[part], lsem.at[h])

    def coef_copy(n):
        return pltpu.make_async_copy(
            coef.at[:, pl.ds(pl.multiple_of(n * CB, CB), CB)], cbuf.at[n], csem.at[n]
        )

    lhs_copy(0).start()
    for n in range(nblk):
        coef_copy(n).start()
    for h in range(1, NCH):
        lhs_copy(h).start()

    bar = pltpu.get_barrier_semaphore()

    def greet(where):
        pl.semaphore_signal(bar, inc=1, device_id=where, device_id_type=MESH)

    def greet_sources(k, carry):
        p, cc = k // 2, k % 2
        greet(dev(x * c + p * (1 - c), y, z * (1 - c) + p * c, cc))
        greet(dev(l, y, p, cc))
        return carry

    lax.fori_loop(0, 8, greet_sources, 0)
    for d in range(1, 4):
        greet(dev((x + d * c) % 4, y, (z + d * (1 - c)) % 4, c))
        greet(dev(x, (y + d) % 4, z, c))

    for b in range(NB):
        for j in range(2):
            for k in range(4):
                p = plist[b, j, k]
                off = jnp.where(p >= 0, p - (2 * t + j) + 2, -1).astype(F32)
                offs[b, pl.ds(4 * j + k, 1)] = jnp.full((1, T), off, F32)

    def start_either(copies):
        far, near, is_self = copies
        if is_self is None:
            far.start()
        else:

            @pl.when(is_self)
            def _():
                near.start()

            @pl.when(jnp.logical_not(is_self))
            def _():
                far.start()

    def finish_send(copies):
        far, near, is_self = copies
        if is_self is None:
            far.wait_send()
        else:

            @pl.when(jnp.logical_not(is_self))
            def _():
                far.wait_send()

    def quarter_of(yy):
        return pl.ds(pl.multiple_of(yy * QR, QR), QR)

    quarter = quarter_of(y)
    me8 = z * 2 + c

    def f1_copies(b, d):
        src = amp.at[b, :, :, quarter]
        dst = ampbuf.at[pl.ds(me8 * 2, 2), :, quarter]
        if b == 0:
            where, is_self = dev(x, y, (z + d) % 4, 0), c == 0
        else:
            where, is_self = dev((x + d) % 4, y, x, 1), (c == 1) & (z == x)
        is_self = is_self if d == 0 else None
        far = remote(src, dst, f1send.at[0, b, d], f1recv.at[0, me8], where)
        near = pltpu.make_async_copy(src, dst, f1recv.at[0, me8])
        far_offs = remote(
            offs.at[b], offbuf.at[me8], f1send.at[1, b, d], f1recv.at[1, me8], where
        )
        near_offs = pltpu.make_async_copy(offs.at[b], offbuf.at[me8], f1recv.at[1, me8])
        return (far_offs, near_offs, is_self), (far, near, is_self)

    def f2_copy(g, kind, receive=False):
        way = 1 - 2 * (kind % 2)
        back = (kind // 2 + (1 if receive else 0)) * way
        slots = pl.ds(4 * g, 4) if kind < 2 else pl.ds(4 * g + 2 * (kind - 2), 2)
        part = ampbuf.at[slots, :, quarter_of((y + 4 - back) % 4)]
        where = here if receive else dev(x, (y + 4 + way) % 4, z, c)
        return remote(part, part, f2send.at[g, kind], f2recv.at[g, kind], where)

    def f2_start(g):
        for k in (2 * g, 2 * g + 1):
            remote(
                offs.at[0], offbuf.at[k], f1send.at[1, 0, 0], f1recv.at[1, k], here
            ).wait_recv()
            remote(
                amp.at[0, :, :, quarter], ampbuf.at[pl.ds(2 * k, 2), :, quarter],
                f1send.at[0, 0, 0], f1recv.at[0, k], here,
            ).wait_recv()
        for kind in range(2):
            f2_copy(g, kind).start()

    def f2_forward(g):
        for kind in range(2):
            f2_copy(g, kind, receive=True).wait_recv()
        for kind in range(2, 4):
            f2_copy(g, kind).start()

    def f2_wait(g):
        for kind in range(2, 4):
            f2_copy(g, kind, receive=True).wait_recv()

    def by_offset(g):
        for e in range(4):
            k8, r = 2 * g + e // 2, 4 * (e % 2)
            for m in range(NOFF):
                total = None
                for k in range(4):
                    row = jnp.broadcast_to(offbuf[k8, pl.ds(r + k, 1)], (16, T))
                    hit = jnp.where(row == float(m), 1.0, 0.0).astype(BF16)
                    term = hit[None] * ampbuf[4 * g + e, k].reshape(T // 16, 16, T)
                    total = term if total is None else total + term
                amp5[4 * g + e, pl.ds(m * T, T)] = total.reshape(T, T)

    def half(h, n):
        rows_h = CHUNKS[h]
        mine = lhs[pl.ds(START[h] * NOCC, rows_h * NOCC)]
        whole = jnp.dot(mine, cbuf[n], preferred_element_type=F32)
        for a in range(CB // T):
            acc[a, pl.ds(0, rows_h * NOCC)] = whole[:, a * T : (a + 1) * T]
        for i in range(NOCC):
            for a in range(CB // T):
                part = acc[a, pl.ds(i, rows_h, stride=NOCC), :]
                if h == NCH - 1:
                    rows = lax.broadcasted_iota(jnp.int32, (rows_h, T), 0)
                    part = jnp.where(rows < tail, part, 0.0)
                ynat[i // 4, (i % 4) * 16 + 2 * n + a, pl.ds(0, rows_h)] = part.astype(BF16)

    def reorder(h):
        for b in range(NB):

            def one(s, carry):
                send[b, s, pl.ds(START[h], CHUNKS[h])] = ynat[
                    b, owned[b, (s + NT - 2) % NT], pl.ds(0, CHUNKS[h])
                ]
                return carry

            lax.fori_loop(0, NT + 4, one, 0, unroll=4)

    def place(h, k):
        rows_h = CHUNKS[h]
        return pl.ds(pl.multiple_of(START[h] * NSRC + k * rows_h, 16), rows_h)

    def part(h):
        return pl.ds(START[h], CHUNKS[h])

    def groups(h):
        return ((0, 8), (8, 4), (12, 4), (16, 4)) if h == NCH - 1 else ((0, WIN),)

    def gather_copies(h, g):
        low, count = groups(h)[g]
        q = h + g
        copies = []
        for d in range(1, 4):
            xd, zd = (x + d) % 4, (z + d) % 4
            for b, at, k, where in (
                (0, xd, x * 2 + c, dev(xd, y, z, 0)),
                (1, zd, z * 2 + c, dev(x, y, zd, 1)),
            ):
                copies.append(
                    remote(
                        send.at[b, pl.ds(at * BLK + low, count), part(h)],
                        recv.at[pl.ds(low, count), place(h, k)],
                        gsend.at[q, len(copies)],
                        grecv.at[q, k],
                        where,
                    )
                )
        copies.append(
            remote(
                send.at[1 - c, pl.ds(o * BLK + low, count), part(h)],
                recv.at[pl.ds(low, count), place(h, o * 2 + c)],
                gsend.at[q, 6],
                grecv.at[q, o * 2 + c],
                dev(x, y, z, 1 - c),
            )
        )
        own = pltpu.make_async_copy(
            send.at[c, pl.ds(l * BLK + low, count), part(h)],
            recv.at[pl.ds(low, count), place(h, l * 2 + c)],
            locsem.at[q],
        )
        return copies, own

    def gather_start(h):
        for g in range(len(groups(h))):
            copies, own = gather_copies(h, g)
            for copy in copies:
                copy.start()
            own.start()

    def gather_wait(h, g):
        low, count = groups(h)[g]
        q = h + g
        gather_copies(h, g)[1].wait()

        def arrived(k):
            remote(
                send.at[0, pl.ds(low, count), part(h)], recv.at[pl.ds(low, count), place(h, k)],
                gsend.at[q, 0], grecv.at[q, k], here,
            ).wait_recv()

        arrived(l * 2 + 1 - c)
        for d in range(1, 4):
            for cc in range(2):
                arrived(((l + d) % 4) * 2 + cc)

    def pairs(low, high, first, last):
        rows = pl.ds(low * NSRC, (high - low) * NSRC)

        def one(j, carry):
            mine = jnp.concatenate([recv[2 * j + 2, rows], recv[2 * j + 3, rows]], axis=1)
            others = jnp.concatenate([recv[2 * j + m, rows] for m in range(6)], axis=1)
            got = lax.dot_general(
                mine, others, (((0,), (0,)), ((), ())), preferred_element_type=F32
            )
            if low == 0:
                rr[j] = got
            else:
                rr[j] = rr[j] + got
            return carry

        lax.fori_loop(first, last, one, 0)

    def contract(g):
        for e in range(4):
            j, u = 2 * g + e // 2, e % 2
            whole = rr[j, pl.ds(u * T, T), pl.ds(u * T, NOFF * T)]
            high = whole.astype(BF16)
            low = (whole - high.astype(F32)).astype(BF16)
            weights = amp5[4 * g + e]
            res[4 * g + e] = jnp.dot(high, weights, preferred_element_type=F32) + jnp.dot(
                low, weights, preferred_element_type=F32
            )

    def first_copy(g, d):
        return remote(
            res.at[4 * g + (o + d) % 4], rsgot.at[g, d - 1], rssend.at[g, d - 1], rsrecv.at[g, d - 1],
            dev((x + d * c) % 4, y, (z + d * (1 - c)) % 4, c),
        )

    def second_copy(g, d):
        return remote(
            ysend.at[g, quarter_of((y + d) % 4)], ygot.at[g, d - 1], yssend.at[g, d - 1],
            ysrecv.at[g, d - 1], dev(x, (y + d) % 4, z, c),
        )

    def second_start(g):
        for d in range(1, 4):
            first_copy(g, d).wait_recv()
        ysend[g] = (res[4 * g + o] + rsgot[g, 0]) + (rsgot[g, 1] + rsgot[g, 2])
        for d in range(1, 4):
            second_copy(g, d).start()

    def final_copies(g, d):
        dst = out.at[c, o % 2, quarter]
        sem = fsrecv.at[c * 8 + (o % 2) * 4 + y]
        far = remote(fsend.at[g], dst, fssend.at[g, d], sem, dev(l, (y + d) % 4, g, o // 2))
        near = pltpu.make_async_copy(fsend.at[g], dst, sem)
        is_self = ((o // 2 == c) & (l == x) & (z == g)) if d == 0 else None
        return far, near, is_self

    def final_start(g):
        for d in range(1, 4):
            second_copy(g, d).wait_recv()
        fsend[g] = (ysend[g, quarter] + ygot[g, 0]) + (ygot[g, 1] + ygot[g, 2])
        for d in range(4):
            start_either(final_copies(g, d))

    def block(h):
        def one(n, carry):
            if h == 0:
                coef_copy(n).wait()
            half(h, n)
            return carry

        return one

    lhs_copy(0).wait()
    pl.semaphore_wait(bar, 22)
    for d in range(4):
        for b in range(NB):
            for one in f1_copies(b, d):
                start_either(one)
    lax.fori_loop(0, nblk, block(0), 0)
    reorder(0)
    gather_start(0)
    lhs_copy(1).wait()
    lax.fori_loop(0, nblk // 2, block(1), 0)
    for g in range(4):
        f2_start(g)
    lax.fori_loop(nblk // 2, nblk, block(1), 0)
    reorder(1)
    gather_start(1)
    lhs_copy(2).wait()
    lax.fori_loop(0, nblk // 2, block(2), 0)
    f2_forward(0)
    lax.fori_loop(nblk // 2, nblk, block(2), 0)
    reorder(2)
    gather_start(2)
    f2_forward(1)
    gather_wait(0, 0)
    pairs(0, START[1], 0, BLK // 2)
    f2_forward(2)
    f2_forward(3)
    gather_wait(1, 0)
    pairs(START[1], START[2], 0, BLK // 2)
    for g in range(4):
        f2_wait(g)
        by_offset(g)
        gather_wait(2, g)
        pairs(START[2], ROWS, 2 * g, 2 * g + 2)
        contract(g)
        for d in range(1, 4):
            first_copy(g, d).start()
    for g in range(4):
        second_start(g)
    for g in range(4):
        final_start(g)

    for b in range(NB):
        for j in range(2):
            for yy in range(4):
                remote(
                    fsend.at[0], out.at[b, j, pl.ds(yy * QR, QR)], fssend.at[0, 0],
                    fsrecv.at[b * 8 + j * 4 + yy], here,
                ).wait_recv()

    for d in range(4):
        for b in range(NB):
            for one in f1_copies(b, d):
                finish_send(one)
    for h in range(NCH):
        for g in range(len(groups(h))):
            for copy in gather_copies(h, g)[0]:
                copy.wait_send()
    for g in range(4):
        for kind in range(4):
            f2_copy(g, kind).wait_send()
        for d in range(1, 4):
            first_copy(g, d).wait_send()
            second_copy(g, d).wait_send()
        for d in range(4):
            finish_send(final_copies(g, d))


def per_device(integrals, coefficients, owned_tiles, pair_list, amplitudes):
    q_rows, occ, ao = integrals.shape
    nv = coefficients.shape[1]
    dma = pltpu.SemaphoreType.DMA
    vmem = pl.BlockSpec(memory_space=pltpu.VMEM)
    smem = pl.BlockSpec(memory_space=pltpu.SMEM)
    hbm = pl.BlockSpec(memory_space=pl.ANY)
    return pl.pallas_call(
        functools.partial(kernel, q_rows),
        out_shape=jax.ShapeDtypeStruct((NB, 2, T, T), F32),
        in_specs=[smem, smem, hbm, hbm, hbm],
        out_specs=vmem,
        scratch_shapes=[
            pltpu.VMEM((ROWS * NOCC, ao), BF16),
            pltpu.VMEM((nv // CB, ao, CB), BF16),
            pltpu.VMEM((CB // T, (max(CHUNKS) + 1) * NOCC, T), F32),
            pltpu.VMEM((NB, NT, max(CHUNKS), T), BF16),
            pltpu.VMEM((NB, NT + 4, ROWS, T), BF16),
            pltpu.VMEM((WIN, NSRC * ROWS, T), BF16),
            pltpu.VMEM((BLK // 2, 2 * T, 6 * T), F32),
            pltpu.VMEM((NB, 8, T), F32),
            pltpu.VMEM((NSRC, 8, T), F32),
            pltpu.VMEM((BLK, NOFF * T, T), BF16),
            pltpu.VMEM((BLK, 4, T, T), BF16),
            pltpu.VMEM((BLK, T, T), F32),
            pltpu.VMEM((4, 3, T, T), F32),
            pltpu.VMEM((4, T, T), F32),
            pltpu.VMEM((4, 3, QR, T), F32),
            pltpu.VMEM((4, QR, T), F32),
            dma((NCH,)),
            dma((nv // CB,)),
            dma((NCH + 3, 7)),
            dma((NCH + 3, NSRC)),
            dma((2, NB, 4)),
            dma((2, NSRC)),
            dma((4, 4)),
            dma((4, 4)),
            dma((4, 3)),
            dma((4, 3)),
            dma((4, 3)),
            dma((4, 3)),
            dma((4, 4)),
            dma((16,)),
            dma((NCH + 3,)),
        ],
        compiler_params=pltpu.CompilerParams(
            collective_id=0, has_side_effects=True, vmem_limit_bytes=60 * 2**20
        ),
        name="residual_kernel",
    )(
        owned_tiles,
        pair_list,
        integrals.reshape(q_rows * occ, ao),
        coefficients,
        amplitudes,
    )


def solution(mesh):
    in_specs = (
        P(("aux", "tile"), None, None),
        P(),
        P(),
        P(None, "tile", None),
        P(None, "tile", None, None, None),
    )
    out_specs = P(None, "tile", None, None)
    return jax.shard_map(
        per_device, mesh=mesh, in_specs=in_specs, out_specs=out_specs, check_vma=False
    )
```
